512 devices in a mesh: seq: 64 (over z, y), head: 8 (over x, core).
Axes of the slice: x: 4, y: 4, z: 16, core: 2. Of those that a mesh axis runs over, the one named last changes fastest.
Arguments:
- queries: bfloat16 [32768, 4096], P('seq', 'head'), may hold values from -64 to 64
- keys: bfloat16 [32768, 2048], P('seq', 'head'), may hold values from -20 to 20
- values: bfloat16 [32768, 2048], P('seq', 'head'), may hold values from -6 to 6
- start_basis: float32 [16, 128, 64], P('head'), may hold values from -6 to 6
- out_weight: bfloat16 [4096, 2688], P('head'), may hold values from -0.09375 to 0.09375
Outputs:
- lowrank_attn: bfloat16 [32768, 4096], P('seq', 'head')
- deviation: bfloat16 [32768, 2688], P(('seq', 'head'))
The draws below stay inside these ranges and needn't reach their ends.
All inputs are finite; a program needn't handle non-finite values.
Results may differ from the reference program's by a relative error of at most 0.029.
Values may be sent and summed in bfloat16 or wider, within the bound.
No kernel may reach another device: no remote copies, remote signals or barrier semaphores. Data moves between devices by JAX's collectives and lax.ppermute only.
A program may use at most 128 MiB of HBM per device.

```python
import math
import jax
import jax.numpy as jnp
from jax import lax

HQ = 32
HK = 16
HD = 128
QSCALE = 168
W = 1024
D_WIN = 2688
RANK = 64
SWEEPS = 8
TOK_DEV = 512
TOKENS = 32768
QH_DEV = 4
N_SEQ = 64
N_HEAD = 8


def key_field(key):
    base_key = jax.random.fold_in(key, 7301)
    key_raw, key_order, key_top, key_bottom, key_mix, key_rough = jax.random.split(base_key, 6)
    raw = jnp.clip(jax.random.normal(key_raw, (TOKENS, HK, HD), jnp.float32), -5.0, 5.0)
    order = jax.vmap(lambda single: jax.random.permutation(single, HD))(jax.random.split(key_order, HK))
    top_spread = jax.random.uniform(key_top, (HK, HD), jnp.float32, 1.0, 1.6)
    bottom_spread = jax.random.uniform(key_bottom, (HK, HD), jnp.float32, 0.55, 0.95)
    spread = jnp.where(order < RANK, top_spread, bottom_spread)
    mixing = jnp.eye(HD, dtype=jnp.float32)[None] + 0.5 / math.sqrt(HD) * jax.random.normal(key_mix, (HK, HD, HD), jnp.float32)
    ramp = 0.6 + 1.2 * jnp.arange(TOKENS, dtype=jnp.float32) / TOKENS
    rough = jnp.exp(jax.random.uniform(key_rough, (TOKENS,), jnp.float32, -0.4, 0.4))
    scaled = raw * spread[None] * (ramp * rough)[:, None, None]
    field = jnp.einsum('thc,hcd->thd', scaled, mixing, precision=lax.Precision.HIGHEST)
    return jnp.clip(field, -20.0, 20.0)


def draw_keys(key, part):
    return key_field(key).reshape(TOKENS, HK * HD).astype(jnp.bfloat16)


def draw_queries(key, part):
    query_key = jax.random.fold_in(key, 9113)
    group_q = HQ // HK
    result = jax.random.normal(query_key, (TOKENS, HK, group_q, HD), jnp.float32)
    return jnp.clip(result, -64.0, 64.0).reshape(TOKENS, HQ * HD).astype(jnp.bfloat16)


def shard_levels(own_key, extent, cuts, low, largest):
    loudness = 1.0
    for axis_at, blocks in cuts:
        heights = jax.random.uniform(jax.random.fold_in(jax.random.fold_in(own_key, 6), axis_at), (blocks,), jnp.float32, low / len(cuts), largest / len(cuts))
        loudness = loudness * jnp.repeat(jnp.exp(heights), extent[axis_at] // blocks).reshape((-1,) + (1,) * (len(extent) - 1 - axis_at))
    return loudness


def noise(own_key, extent, deviation, reach, cuts=(), kind=jnp.bfloat16):
    drawn = jax.random.normal(own_key, extent, jnp.float32) * deviation
    if len(cuts) > 0:
        drawn = shard_levels(own_key, extent, cuts, -0.22, 0.18) * drawn
    return jnp.clip(drawn, min=-reach, max=reach).astype(kind)


def setup_inputs(seed: int = 0) -> dict:
    key_list = jax.random.split(jax.random.key(seed), 6)
    return {
        "queries": draw_queries(jax.random.fold_in(key_list[5], 71), 0),
        "keys": draw_keys(jax.random.fold_in(key_list[5], 71), 0),
        "values": noise(key_list[2], (TOKENS, HK * HD), 1.0, 6.0, ((0, 64), (1, 8))),
        "start_basis": noise(key_list[3], (HK, HD, RANK), 1.0, 6.0, ((0, 8),), jnp.float32),
        "out_weight": noise(key_list[4], (HQ * HD, D_WIN), (HQ * HD) ** -0.5, 0.09375, ((0, 8),)),
    }


HIGHEST = lax.Precision.HIGHEST
NEGLIGIBLE = -1e+30

def orthonormal(columns):
    inner_prod = jnp.einsum('hcr,hcq->hrq', columns, columns, precision=HIGHEST)
    factor_low = jnp.linalg.cholesky(inner_prod)

    def solve_one(factor, column):
        return jax.scipy.linalg.solve_triangular(factor, column.T, lower=True).T
    return jax.vmap(solve_one)(factor_low, columns)

def attend(query_rows, key_rows, value_rows, first_pos, score_scale):
    row_count = query_rows.shape[0]
    key_span = key_rows.shape[0]
    query_pos = first_pos + jnp.arange(row_count, dtype=jnp.int32)
    key_pos = first_pos + row_count - key_span + jnp.arange(key_span, dtype=jnp.int32)
    allowed = (key_pos[None, :] >= 0) & (key_pos[None, :] <= query_pos[:, None]) & (query_pos[:, None] - key_pos[None, :] < W)
    scores = jnp.einsum('thgd,shd->hgts', query_rows.astype(jnp.float32), key_rows.astype(jnp.float32), precision=HIGHEST) * score_scale
    scores = jnp.where(allowed, scores, NEGLIGIBLE)
    row_peak = jnp.max(scores, axis=-1, keepdims=True)
    raised = jnp.exp(scores - row_peak)
    weights = (raised / jnp.sum(raised, axis=-1, keepdims=True)).astype(jnp.bfloat16)
    return jnp.einsum('hgts,shd->thgd', weights.astype(jnp.float32), value_rows.astype(jnp.float32), precision=HIGHEST)

def reference(queries, keys, values, start_basis, out_weight):
    group_q = HQ // HK
    score_scale = QSCALE ** (-0.5)
    key_heads = keys.reshape(TOKENS, HK, HD)
    value_heads = values.reshape(TOKENS, HK, HD)
    query_heads = queries.reshape(TOKENS, HK, group_q, HD)
    key_float = key_heads.astype(jnp.float32)
    key_gram = jnp.einsum('thc,thd->hcd', key_float, key_float, precision=HIGHEST)
    basis = start_basis
    for sweep in range(SWEEPS):
        basis = orthonormal(jnp.einsum('hcd,hdr->hcr', key_gram, basis, precision=HIGHEST))
    basis_half = basis.astype(jnp.bfloat16)
    query_low = jnp.einsum('thgc,hcr->thgr', query_heads.astype(jnp.float32), basis_half.astype(jnp.float32), precision=HIGHEST).astype(jnp.bfloat16)
    key_low = jnp.einsum('thc,hcr->thr', key_float, basis_half.astype(jnp.float32), precision=HIGHEST).astype(jnp.bfloat16)
    key_pad = jnp.concatenate([jnp.zeros((W, HK, HD), jnp.bfloat16), key_heads], axis=0)
    low_pad = jnp.concatenate([jnp.zeros((W, HK, RANK), jnp.bfloat16), key_low], axis=0)
    value_pad = jnp.concatenate([jnp.zeros((W, HK, HD), jnp.bfloat16), value_heads], axis=0)

    def one_block(index):
        first_pos = (index * TOK_DEV).astype(jnp.int32)
        query_rows = lax.dynamic_slice_in_dim(query_heads, first_pos, TOK_DEV, 0)
        query_lrows = lax.dynamic_slice_in_dim(query_low, first_pos, TOK_DEV, 0)
        key_rows = lax.dynamic_slice_in_dim(key_pad, first_pos, W + TOK_DEV, 0)
        key_lrows = lax.dynamic_slice_in_dim(low_pad, first_pos, W + TOK_DEV, 0)
        value_rows = lax.dynamic_slice_in_dim(value_pad, first_pos, W + TOK_DEV, 0)
        exact = attend(query_rows, key_rows, value_rows, first_pos, score_scale)
        approx = attend(query_lrows, key_lrows, value_rows, first_pos, score_scale)
        return (approx.astype(jnp.bfloat16), (exact - approx).astype(jnp.bfloat16))
    approx_all, gap_all = lax.map(one_block, jnp.arange(N_SEQ, dtype=jnp.int32))
    lowrank_attn = approx_all.reshape(TOKENS, HQ * HD)
    gap = gap_all.reshape(TOKENS, HQ * HD)
    group_width = QH_DEV * HD
    total = jnp.zeros((TOKENS, D_WIN), jnp.float32)
    for group in range(N_HEAD):
        partial_value = jnp.dot(gap[:, group * group_width:(group + 1) * group_width].astype(jnp.float32), out_weight[group * group_width:(group + 1) * group_width].astype(jnp.float32), preferred_element_type=jnp.float32).astype(jnp.bfloat16)
        partial_value = lax.optimization_barrier(partial_value)
        total = total + partial_value.astype(jnp.float32)
    return (lowrank_attn, total.astype(jnp.bfloat16))
```

```python
import functools

import jax
import jax.numpy as jnp
from jax import lax
from jax.experimental import pallas as pl
from jax.experimental.pallas import tpu as pltpu
from jax.sharding import Mesh
from jax.sharding import PartitionSpec as P

HD = 128
QSCALE = 168
RANK = 64
TOK = 512
QB = 256
NZ, NY, NX = 16, 4, 4

HIGHEST = lax.Precision.HIGHEST
EXP2_SCALE = QSCALE**-0.5 * 1.4426950408889634
BIG = 1e30
F32, BF16 = jnp.float32, jnp.bfloat16

PLAN = (1, 1, 2, 2, 2)


def nt(a, b, precision=None):
    return lax.dot_general(a, b, (((1,), (1,)), ((), ())), precision=precision, preferred_element_type=F32)


def nn(a, b, precision=None):
    return lax.dot_general(a, b, (((1,), (0,)), ((), ())), precision=precision, preferred_element_type=F32)


def orthonormal_rows(rows_list):
    nb = 8
    groups = RANK // nb
    lane_shape = (nb, 2 * RANK)
    sub = lax.broadcasted_iota(jnp.int32, lane_shape, 0)
    eye = (
        lax.broadcasted_iota(jnp.int32, (RANK, RANK), 0)
        == lax.broadcasted_iota(jnp.int32, (RANK, RANK), 1)
    ).astype(F32)
    tables = []
    for z in rows_list:
        both = jnp.concatenate([nt(z, z, HIGHEST), eye], axis=1)
        tables.append([both[nb * g : nb * g + nb] for g in range(groups)])
    for g0 in range(groups):
        k0 = nb * g0
        for table in tables:
            rows = [jnp.broadcast_to(table[g0][j : j + 1, :], lane_shape) for j in range(nb)]
            cols = [
                [jnp.broadcast_to(table[g][:, k0 + j : k0 + j + 1], lane_shape) for g in range(g0, groups)]
                for j in range(nb)
            ]
            inner = [
                [jnp.broadcast_to(cols[j][0][i : i + 1, :], lane_shape) if j >= i else None for j in range(nb)]
                for i in range(nb)
            ]
            pivots = []
            for j in range(nb):
                inv = lax.rsqrt(inner[j][j])
                row = rows[j] * inv
                col = [c * inv for c in cols[j]]
                pivots.append((row, col))
                factors = [inner[j][k] * inv if k >= j else None for k in range(nb)]
                for k in range(j + 1, nb):
                    rows[k] = rows[k] - factors[k] * row
                    cols[k] = [a - b * factors[k] for a, b in zip(cols[k], col)]
                    for m in range(k, nb):
                        inner[k][m] = inner[k][m] - factors[k] * factors[m]
            for at, g in enumerate(range(g0, groups)):
                x = table[g]
                for j, (row, col) in enumerate(pivots):
                    less = x - col[at] * row
                    x = jnp.where(sub > j, less, jnp.where(sub == j, row, x)) if g == g0 else less
                table[g] = x
    return [
        nn(jnp.concatenate(table, axis=0)[:, RANK:], z, HIGHEST) for table, z in zip(tables, rows_list)
    ]


def basis_kernel(gram_ref, start_ref, out_ref, rows_ref, powers_ref):
    heads = gram_ref.shape[0]
    for h in range(heads):
        gram = gram_ref[h]
        powers_ref[0, h] = gram
        powers_ref[1, h] = nn(gram, gram, HIGHEST)
        rows_ref[h] = start_ref[h].T
    singles = sum(1 for p in PLAN if p == 1)

    def step(i, carry):
        power = (i >= singles).astype(jnp.int32)
        moved = [nn(rows_ref[h], powers_ref[power, h], HIGHEST) for h in range(heads)]
        for h, rows in enumerate(orthonormal_rows(moved)):
            rows_ref[h] = rows
        return carry

    lax.fori_loop(0, len(PLAN), step, 0)
    for h in range(heads):
        out_ref[h] = rows_ref[h].T.astype(BF16)


def find_basis(gram, start):
    heads = gram.shape[0]
    return pl.pallas_call(
        basis_kernel,
        name="basis",
        out_shape=jax.ShapeDtypeStruct((heads, HD, RANK), BF16),
        scratch_shapes=[
            pltpu.VMEM((heads, RANK, HD), F32),
            pltpu.VMEM((2, heads, HD, HD), F32),
        ],
        compiler_params=pltpu.CompilerParams(vmem_limit_bytes=16 << 20),
        cost_estimate=pl.CostEstimate(flops=40_000_000, bytes_accessed=400_000, transcendentals=0),
    )(gram, start)


def attend(q, keys, vals, bias):
    row = lax.broadcasted_iota(jnp.int32, (QB, QB), 0)
    col = lax.broadcasted_iota(jnp.int32, (QB, QB), 1)
    old = col > row
    scores = [jnp.where(old, nt(q, keys[0]) + bias[0], nt(q, keys[4]))]
    scores += [nt(q, keys[b]) for b in (1, 2, 3)]
    peak = jnp.maximum(scores[0][:, :128], scores[0][:, 128:])
    for b in (1, 2, 3):
        peak = jnp.maximum(peak, jnp.maximum(scores[b][:, :128], scores[b][:, 128:]) + bias[b])
    peak = jnp.max(peak, axis=1, keepdims=True)
    edge = jnp.exp2((scores[0] - peak) * EXP2_SCALE)
    total = nn(jnp.where(old, edge, 0.0).astype(BF16), vals[0])
    total += nn(jnp.where(old, 0.0, edge).astype(BF16), vals[4])
    for b in (1, 2, 3):
        total += nn(jnp.exp2((scores[b] - (peak - bias[b])) * EXP2_SCALE).astype(BF16), vals[b])
    return total[:, :HD] / total[:, HD:]


def window_blocks(block_ref, k_ref, v_ref, near_ref, far_ref):
    first_valid = 4 - 2 * block_ref[0]
    ones = jnp.ones((QB, HD), BF16)
    keys, vals, bias = [], [], []
    for w in range(6):
        at = slice(w % 2 * QB, w % 2 * QB + QB)
        if w < 4:
            source = (far_ref, near_ref)[w // 2]
            key, val = source[0, at, :], source[1, at, :]
        else:
            key, val = k_ref[at, :], v_ref[at, :]
        keys.append(key)
        vals.append(jnp.concatenate([val, ones], axis=1))
        bias.append(jnp.where(w < first_valid, -BIG, 0.0).astype(F32))
    return keys, vals, bias


def tiles():
    for qb in range(TOK // QB):
        for j in range(2):
            yield qb, slice(qb * QB, (qb + 1) * QB), slice(j * HD, (j + 1) * HD)


def exact_kernel(block_ref, q_ref, k_ref, v_ref, near_ref, far_ref, out_ref):
    keys, vals, bias = window_blocks(block_ref, k_ref, v_ref, near_ref, far_ref)
    for qb, rows, cols in tiles():
        out_ref[rows, cols] = attend(q_ref[rows, cols], keys[qb : qb + 5], vals[qb : qb + 5], bias[qb:])


def approx_kernel(block_ref, q_ref, k_ref, v_ref, near_ref, far_ref, basis_ref, exact_ref, low_ref, gap_ref):
    keys, vals, bias = window_blocks(block_ref, k_ref, v_ref, near_ref, far_ref)
    basis = basis_ref[0]
    keys = [nn(key, basis).astype(BF16) for key in keys]
    for qb, rows, cols in tiles():
        q = nn(q_ref[rows, cols], basis).astype(BF16)
        approx = attend(q, keys[qb : qb + 5], vals[qb : qb + 5], bias[qb:])
        low_ref[rows, cols] = approx.astype(BF16)
        gap_ref[rows, cols] = (exact_ref[rows, cols] - approx).astype(BF16)


PAIR = pl.BlockSpec((TOK, 2 * HD), lambda h, block: (0, h))
ONE = pl.BlockSpec((TOK, HD), lambda h, block: (0, h))
BOTH = pl.BlockSpec((2, TOK, HD), lambda h, block: (0, 0, h))
BASIS = pl.BlockSpec((1, HD, RANK), lambda h, block: (h, 0, 0))
ATTEND_COST = pl.CostEstimate(flops=4 * TOK * 1280 * 512, bytes_accessed=4 << 20, transcendentals=4 * TOK * 1024)


def attention(kernel, name, in_specs, out_shape, operands):
    heads = operands[2].shape[1] // HD
    return pl.pallas_call(
        kernel,
        name=name,
        out_shape=out_shape,
        grid_spec=pltpu.PrefetchScalarGridSpec(
            num_scalar_prefetch=1,
            grid=(heads,),
            in_specs=in_specs,
            out_specs=jax.tree.map(lambda _: PAIR, out_shape),
        ),
        compiler_params=pltpu.CompilerParams(vmem_limit_bytes=40 << 20),
        cost_estimate=ATTEND_COST,
    )(*operands)


def shards(queries, keys, values, start_basis, out_weight):
    z, y = lax.axis_index("z"), lax.axis_index("y")
    core = lax.axis_index("core")
    block = (z * NY + y).astype(jnp.int32).reshape(1)

    paired = jnp.stack([keys, values])
    seq = NZ * NY
    near = lax.ppermute(paired, ("z", "y"), [(i, i + 1) for i in range(seq - 1)])
    far = lax.ppermute(paired, ("z", "y"), [(i, i + 2) for i in range(seq - 2)])
    swap = [(0, 1), (1, 0)]
    their_weight = lax.ppermute(out_weight, "core", swap)

    key_heads = keys.reshape(TOK, -1, HD)
    gram = jnp.einsum("thc,thd->hcd", key_heads, key_heads, preferred_element_type=F32)
    shape = gram.shape
    gram = lax.all_to_all(gram.reshape(NY, -1, HD), "y", 0, 0, tiled=True).sum(0)
    for bit in (1, 2, 4, 8):
        gram = gram + lax.ppermute(gram, "z", [(i, i ^ bit) for i in range(NZ)])
    gram = jnp.broadcast_to(gram[None], (NY,) + gram.shape)
    gram = lax.all_to_all(gram, "y", 0, 0, tiled=True).reshape(shape)

    window = (block, queries, keys, values, near, far)
    specs = [PAIR, ONE, ONE, BOTH, BOTH]
    exact = attention(exact_kernel, "exact", specs, jax.ShapeDtypeStruct(queries.shape, F32), window)
    basis_half = find_basis(gram, start_basis)
    low = jax.ShapeDtypeStruct(queries.shape, BF16)
    lowrank_attn, gap = attention(
        approx_kernel, "approx", specs + [BASIS, PAIR], [low, low], window + (basis_half, exact)
    )

    width = gap.shape[1]
    chunk = TOK // (2 * NX)
    by_core = gap.reshape(NX, 2, chunk, width)
    mine = lax.dynamic_index_in_dim(by_core, core, 1, False).reshape(-1, width)
    theirs = lax.dynamic_index_in_dim(by_core, 1 - core, 1, False).reshape(-1, width)
    theirs = lax.ppermute(theirs, "core", swap)
    partial = jnp.dot(mine, out_weight, preferred_element_type=F32)
    partial += jnp.dot(theirs, their_weight, preferred_element_type=F32)
    partial = partial.astype(BF16).reshape(NX, chunk, -1)
    partial = lax.all_to_all(partial, "x", 0, 0, tiled=True)
    deviation = partial.astype(F32).sum(0).astype(BF16)
    return lowrank_attn, deviation


def solution(mesh):
    fine = Mesh(mesh.devices.reshape(NZ, NY, NX, 2), ("z", "y", "x", "core"))
    seq, head = ("z", "y"), ("x", "core")
    placed = (P(seq, head), P(seq, head), P(seq, head), P(head, None, None), P(head, None))
    return jax.shard_map(
        shards,
        mesh=fine,
        in_specs=placed,
        out_specs=(P(seq, head), P(seq + head, None)),
        check_vma=False,
    )
```

```python
import jax
import jax.numpy as jnp
from jax import lax
from jax.experimental import pallas as pl
from jax.experimental.pallas import tpu as pltpu
from jax.sharding import Mesh
from jax.sharding import PartitionSpec as P

HD = 128
QSCALE = 168
RANK = 64
TOK = 512
QB = 256
NZ, NY, NX = 16, 4, 4
QUARTER = HD // NY
PIECE = QUARTER + 8
CHUNK = TOK // (2 * NX)
SPLIT = 1280

HIGHEST = lax.Precision.HIGHEST
EXP2_SCALE = QSCALE**-0.5 * 1.4426950408889634
BIG = 1e30
F32, BF16 = jnp.float32, jnp.bfloat16

PLAN = (1, 1, 2, 2, 2)


def nt(a, b, precision=None):
    return lax.dot_general(a, b, (((1,), (1,)), ((), ())), precision=precision, preferred_element_type=F32)


def nn(a, b, precision=None):
    return lax.dot_general(a, b, (((1,), (0,)), ((), ())), precision=precision, preferred_element_type=F32)


def orthonormal_rows(rows_list):
    nb = 8
    groups = RANK // nb
    lane_shape = (nb, 2 * RANK)
    sub = lax.broadcasted_iota(jnp.int32, lane_shape, 0)
    eye = (
        lax.broadcasted_iota(jnp.int32, (RANK, RANK), 0)
        == lax.broadcasted_iota(jnp.int32, (RANK, RANK), 1)
    ).astype(F32)
    tables = []
    for z in rows_list:
        both = jnp.concatenate([nt(z, z, HIGHEST), eye], axis=1)
        tables.append([both[nb * g : nb * g + nb] for g in range(groups)])
    for g0 in range(groups):
        k0 = nb * g0
        for table in tables:
            rows = [jnp.broadcast_to(table[g0][j : j + 1, :], lane_shape) for j in range(nb)]
            cols = [
                [jnp.broadcast_to(table[g][:, k0 + j : k0 + j + 1], lane_shape) for g in range(g0, groups)]
                for j in range(nb)
            ]
            inner = [
                [jnp.broadcast_to(cols[j][0][i : i + 1, :], lane_shape) if j >= i else None for j in range(nb)]
                for i in range(nb)
            ]
            pivots = []
            for j in range(nb):
                inv = lax.rsqrt(inner[j][j])
                row = rows[j] * inv
                col = [c * inv for c in cols[j]]
                pivots.append((row, col))
                factors = [inner[j][k] * inv if k >= j else None for k in range(nb)]
                for k in range(j + 1, nb):
                    rows[k] = rows[k] - factors[k] * row
                    cols[k] = [a - b * factors[k] for a, b in zip(cols[k], col)]
                    for m in range(k, nb):
                        inner[k][m] = inner[k][m] - factors[k] * factors[m]
            for at, g in enumerate(range(g0, groups)):
                x = table[g]
                for j, (row, col) in enumerate(pivots):
                    less = x - col[at] * row
                    x = jnp.where(sub > j, less, jnp.where(sub == j, row, x)) if g == g0 else less
                table[g] = x
    return [
        nn(jnp.concatenate(table, axis=0)[:, RANK:], z, HIGHEST) for table, z in zip(tables, rows_list)
    ]


def gram_kernel(k_ref, out_ref):
    grams = []
    for h in range(2):
        k = k_ref[:, h * HD : (h + 1) * HD]
        grams.append(lax.dot_general(k, k, (((0,), (0,)), ((), ())), preferred_element_type=F32))
    row = lax.broadcasted_iota(jnp.int32, (HD, HD), 0)
    col = lax.broadcasted_iota(jnp.int32, (HD, HD), 1)
    packed = jnp.where(col >= row, grams[0], grams[1])
    diagonal = jnp.sum(jnp.where(row == col, grams[1], 0.0), axis=0, keepdims=True)
    for q in range(NY):
        out_ref[q, :QUARTER, :] = packed[q * QUARTER : (q + 1) * QUARTER]
        out_ref[q, QUARTER:, :] = jnp.broadcast_to(diagonal, (PIECE - QUARTER, HD))


def pack_gram(keys):
    return pl.pallas_call(
        gram_kernel,
        name="gram",
        out_shape=jax.ShapeDtypeStruct((NY, PIECE, HD), F32),
        compiler_params=pltpu.CompilerParams(vmem_limit_bytes=8 << 20),
        cost_estimate=pl.CostEstimate(flops=4 * TOK * HD * HD, bytes_accessed=400_000, transcendentals=0),
    )(keys)


def basis_kernel(packed_ref, start_ref, out_ref, rows_ref, powers_ref):
    heads = start_ref.shape[0]
    row = lax.broadcasted_iota(jnp.int32, (HD, HD), 0)
    col = lax.broadcasted_iota(jnp.int32, (HD, HD), 1)
    packed = jnp.concatenate([packed_ref[q, :QUARTER, :] for q in range(NY)], axis=0)
    turned = packed.T
    diagonal = packed_ref[0, QUARTER : QUARTER + 1, :]
    grams = (
        jnp.where(col >= row, packed, turned),
        jnp.where(col < row, packed, jnp.where(row == col, diagonal, turned)),
    )
    for h in range(heads):
        powers_ref[0, h] = grams[h]
        powers_ref[1, h] = nn(grams[h], grams[h], HIGHEST)
        rows_ref[h] = start_ref[h].T
    singles = sum(1 for p in PLAN if p == 1)

    def step(i, carry):
        power = (i >= singles).astype(jnp.int32)
        moved = [nn(rows_ref[h], powers_ref[power, h], HIGHEST) for h in range(heads)]
        for h, rows in enumerate(orthonormal_rows(moved)):
            rows_ref[h] = rows
        return carry

    lax.fori_loop(0, len(PLAN), step, 0)
    for h in range(heads):
        out_ref[h] = rows_ref[h].T.astype(BF16)


def find_basis(packed, start):
    heads = start.shape[0]
    return pl.pallas_call(
        basis_kernel,
        name="basis",
        out_shape=jax.ShapeDtypeStruct((heads, HD, RANK), BF16),
        scratch_shapes=[
            pltpu.VMEM((heads, RANK, HD), F32),
            pltpu.VMEM((2, heads, HD, HD), F32),
        ],
        compiler_params=pltpu.CompilerParams(vmem_limit_bytes=8 << 20),
        cost_estimate=pl.CostEstimate(flops=40_000_000, bytes_accessed=400_000, transcendentals=0),
    )(packed, start)


def attend(q, keys, vals, bias):
    row = lax.broadcasted_iota(jnp.int32, (QB, QB), 0)
    col = lax.broadcasted_iota(jnp.int32, (QB, QB), 1)
    old = col > row
    scores = [jnp.where(old, nt(q, keys[0]) + bias[0], nt(q, keys[4]))]
    scores += [nt(q, keys[b]) for b in (1, 2, 3)]
    peak = jnp.maximum(scores[0][:, :128], scores[0][:, 128:])
    for b in (1, 2, 3):
        peak = jnp.maximum(peak, jnp.maximum(scores[b][:, :128], scores[b][:, 128:]) + bias[b])
    peak = jnp.max(peak, axis=1, keepdims=True)
    edge = jnp.exp2((scores[0] - peak) * EXP2_SCALE)
    total = nn(jnp.where(old, edge, 0.0).astype(BF16), vals[0])
    total += nn(jnp.where(old, 0.0, edge).astype(BF16), vals[4])
    for b in (1, 2, 3):
        total += nn(jnp.exp2((scores[b] - (peak - bias[b])) * EXP2_SCALE).astype(BF16), vals[b])
    return total[:, :HD] / total[:, HD:]


def window_blocks(at_ref, k_ref, v_ref, near_ref, far_ref):
    first_valid = 4 - 2 * at_ref[0]
    ones = jnp.ones((QB, HD), BF16)
    keys, vals, bias = [], [], []
    for w in range(6):
        at = slice(w % 2 * QB, w % 2 * QB + QB)
        if w < 4:
            source = (far_ref, near_ref)[w // 2]
            key, val = source[0, at, :], source[1, at, :]
        else:
            key, val = k_ref[at, :], v_ref[at, :]
        keys.append(key)
        vals.append(jnp.concatenate([val, ones], axis=1))
        bias.append(jnp.where(w < first_valid, -BIG, 0.0).astype(F32))
    return keys, vals, bias


def attention_kernel(at_ref, q_ref, k_ref, v_ref, near_ref, far_ref, basis_ref, low_ref, mine_ref, theirs_ref):
    keys, vals, bias = window_blocks(at_ref, k_ref, v_ref, near_ref, far_ref)
    basis = basis_ref[0]
    low_keys = [nn(key, basis).astype(BF16) for key in keys]
    away = [(i + NX - at_ref[2]) & (NX - 1) for i in range(NX)]
    slots = [jnp.where(d == 0, 3, jnp.where(d == 2, 0, jnp.where(d == 1, 1, 2))) for d in away]
    for qb in range(TOK // QB):
        rows = slice(qb * QB, (qb + 1) * QB)
        span = slice(qb, qb + 5)
        for j in range(2):
            cols = slice(j * HD, (j + 1) * HD)
            q = q_ref[rows, cols]
            exact = attend(q, keys[span], vals[span], bias[qb:])
            approx = attend(nn(q, basis).astype(BF16), low_keys[span], vals[span], bias[qb:])
            low_ref[rows, cols] = approx.astype(BF16)
            gap = (exact - approx).astype(BF16)
            for i in range(QB // (2 * CHUNK)):
                first = gap[2 * i * CHUNK : (2 * i + 1) * CHUNK]
                second = gap[(2 * i + 1) * CHUNK : (2 * i + 2) * CHUNK]
                slot = slots[qb * (NX // 2) + i]
                to = pl.ds(pl.multiple_of(slot * CHUNK, CHUNK), CHUNK)
                mine_ref[to, cols] = jnp.where(at_ref[1] == 0, first, second)
                theirs_ref[to, cols] = jnp.where(at_ref[1] == 0, second, first)


def attention(at, queries, keys, values, near, far, basis):
    heads = basis.shape[0]
    pair = pl.BlockSpec((TOK, 2 * HD), lambda h, at: (0, h))
    one = pl.BlockSpec((TOK, HD), lambda h, at: (0, h))
    both = pl.BlockSpec((2, TOK, HD), lambda h, at: (0, 0, h))
    half = pl.BlockSpec((TOK // 2, 2 * HD), lambda h, at: (0, h))
    low = jax.ShapeDtypeStruct(queries.shape, BF16)
    gap = jax.ShapeDtypeStruct((TOK // 2, queries.shape[1]), BF16)
    return pl.pallas_call(
        attention_kernel,
        name="attention",
        out_shape=[low, gap, gap],
        grid_spec=pltpu.PrefetchScalarGridSpec(
            num_scalar_prefetch=1,
            grid=(heads,),
            in_specs=[pair, one, one, both, both, pl.BlockSpec((1, HD, RANK), lambda h, at: (h, 0, 0))],
            out_specs=[pair, half, half],
        ),
        compiler_params=pltpu.CompilerParams(vmem_limit_bytes=32 << 20),
        cost_estimate=pl.CostEstimate(
            flops=8 * TOK * 1280 * 512, bytes_accessed=6 << 20, transcendentals=8 * TOK * 1024
        ),
    )(at, queries, keys, values, near, far, basis)


def shards(queries, keys, values, start_basis, out_weight):
    z, y, x = (lax.axis_index(name).astype(jnp.int32) for name in ("z", "y", "x"))
    core = lax.axis_index("core").astype(jnp.int32)
    swap = [(0, 1), (1, 0)]

    gram = lax.all_to_all(pack_gram(keys), "y", 0, 0, tiled=True).sum(0)
    paired = jnp.stack([keys, values])
    gram, paired = lax.optimization_barrier((gram, paired))

    passed = lax.ppermute(paired, "y", [(i, (i - 1) % NY) for i in range(NY)])
    for bit in (1, 2, 4, 8):
        gram = gram + lax.ppermute(gram, "z", [(i, i ^ bit) for i in range(NZ)])
    gram = lax.all_to_all(jnp.broadcast_to(gram[None], (NY,) + gram.shape), "y", 0, 0, tiled=True)
    gram, paired, passed, out_weight = lax.optimization_barrier((gram, paired, passed, out_weight))

    seq = NZ * NY
    near = lax.ppermute(paired, ("z", "y"), [(i, i + 1) for i in range(seq - 1)])
    holder = lambda i: i - 1 if i % NY else i + NY - 1
    far = lax.ppermute(passed, ("z", "y"), [(holder(i), i + 2) for i in range(seq - 2)])
    other_weight = lax.ppermute(out_weight, "core", swap)
    basis_half = find_basis(gram, start_basis)

    at = jnp.stack([z * NY + y, core, x])
    in_place = lambda array: pltpu.with_memory_space_constraint(array, pltpu.HBM)
    lowrank_attn, mine, theirs = attention(at, *map(in_place, (queries, keys, values)), near, far, basis_half)

    theirs = lax.ppermute(theirs, "core", swap)

    def project(rows):
        total = jnp.dot(mine[rows], out_weight, preferred_element_type=F32)
        return (total + jnp.dot(theirs[rows], other_weight, preferred_element_type=F32)).astype(BF16)

    up = lambda part: lax.ppermute(part, "x", [(i, (i + 1) % NX) for i in range(NX)])
    down = lambda part: lax.ppermute(part, "x", [(i, (i - 1) % NX) for i in range(NX)])
    add = lambda *parts: sum(part.astype(F32) for part in parts)
    low, high = slice(0, SPLIT), slice(SPLIT, None)
    across = project(slice(0, CHUNK))
    passed_up, passed_down = up(across[:, low]), down(across[:, high])
    rest = project(slice(CHUNK, None))
    above, below, here = (rest[i * CHUNK : (i + 1) * CHUNK] for i in range(3))
    up_high, down_low = up(above[:, high]), down(below[:, low])
    up_low = up(add(above[:, low], passed_up).astype(BF16))
    down_high = down(add(below[:, high], passed_down).astype(BF16))
    deviation = [
        add(here[:, low], up_low, down_low).astype(BF16),
        add(here[:, high], up_high, down_high).astype(BF16),
    ]
    return lowrank_attn, jnp.concatenate(deviation, axis=1)


def solution(mesh):
    fine = Mesh(mesh.devices.reshape(NZ, NY, NX, 2), ("z", "y", "x", "core"))
    seq, head = ("z", "y"), ("x", "core")
    placed = (P(seq, head), P(seq, head), P(seq, head), P(head, None, None), P(head, None))
    return jax.shard_map(
        shards,
        mesh=fine,
        in_specs=placed,
        out_specs=(P(seq, head), P(seq + head, None)),
        check_vma=False,
    )
```

```python
import jax
import jax.numpy as jnp
from jax import lax
from jax.experimental import pallas as pl
from jax.experimental.pallas import tpu as pltpu
from jax.sharding import Mesh
from jax.sharding import PartitionSpec as P

HD = 128
QSCALE = 168
RANK = 64
TOK = 512
QB = 256
NZ, NY, NX = 16, 4, 4
CHUNK = TOK // (2 * NX)

HIGHEST = lax.Precision.HIGHEST
EXP2_SCALE = QSCALE**-0.5 * 1.4426950408889634
BIG = 1e30
F32, BF16 = jnp.float32, jnp.bfloat16

PLAN = (1, 1, 2, 2, 2)


def nt(a, b, precision=None):
    return lax.dot_general(a, b, (((1,), (1,)), ((), ())), precision=precision, preferred_element_type=F32)


def nn(a, b, precision=None):
    return lax.dot_general(a, b, (((1,), (0,)), ((), ())), precision=precision, preferred_element_type=F32)


def orthonormal_rows(rows_list):
    nb = 8
    groups = RANK // nb
    lane_shape = (nb, 2 * RANK)
    sub = lax.broadcasted_iota(jnp.int32, lane_shape, 0)
    eye = (
        lax.broadcasted_iota(jnp.int32, (RANK, RANK), 0)
        == lax.broadcasted_iota(jnp.int32, (RANK, RANK), 1)
    ).astype(F32)
    tables = []
    for z in rows_list:
        both = jnp.concatenate([nt(z, z, HIGHEST), eye], axis=1)
        tables.append([both[nb * g : nb * g + nb] for g in range(groups)])
    for g0 in range(groups):
        k0 = nb * g0
        for table in tables:
            rows = [jnp.broadcast_to(table[g0][j : j + 1, :], lane_shape) for j in range(nb)]
            cols = [
                [jnp.broadcast_to(table[g][:, k0 + j : k0 + j + 1], lane_shape) for g in range(g0, groups)]
                for j in range(nb)
            ]
            inner = [
                [jnp.broadcast_to(cols[j][0][i : i + 1, :], lane_shape) if j >= i else None for j in range(nb)]
                for i in range(nb)
            ]
            pivots = []
            for j in range(nb):
                inv = lax.rsqrt(inner[j][j])
                row = rows[j] * inv
                col = [c * inv for c in cols[j]]
                pivots.append((row, col))
                factors = [inner[j][k] * inv if k >= j else None for k in range(nb)]
                for k in range(j + 1, nb):
                    rows[k] = rows[k] - factors[k] * row
                    cols[k] = [a - b * factors[k] for a, b in zip(cols[k], col)]
                    for m in range(k, nb):
                        inner[k][m] = inner[k][m] - factors[k] * factors[m]
            for at, g in enumerate(range(g0, groups)):
                x = table[g]
                for j, (row, col) in enumerate(pivots):
                    less = x - col[at] * row
                    x = jnp.where(sub > j, less, jnp.where(sub == j, row, x)) if g == g0 else less
                table[g] = x
    return [
        nn(jnp.concatenate(table, axis=0)[:, RANK:], z, HIGHEST) for table, z in zip(tables, rows_list)
    ]


def basis_kernel(gram_ref, start_ref, out_ref, rows_ref, powers_ref):
    heads = start_ref.shape[0]
    grams = [gram_ref[h] for h in range(heads)]
    for h in range(heads):
        powers_ref[0, h] = grams[h]
        powers_ref[1, h] = nn(grams[h], grams[h], HIGHEST)
        rows_ref[h] = start_ref[h]
    singles = sum(1 for p in PLAN if p == 1)

    def step(i, carry):
        power = (i >= singles).astype(jnp.int32)
        moved = [nn(rows_ref[h], powers_ref[power, h], HIGHEST) for h in range(heads)]
        for h, rows in enumerate(orthonormal_rows(moved)):
            rows_ref[h] = rows
        return carry

    lax.fori_loop(0, len(PLAN), step, 0)
    for h in range(heads):
        out_ref[h] = rows_ref[h].T.astype(BF16)


def find_basis(gram, start):
    heads = start.shape[0]
    return pl.pallas_call(
        basis_kernel,
        name="basis",
        out_shape=jax.ShapeDtypeStruct((heads, HD, RANK), BF16),
        scratch_shapes=[
            pltpu.VMEM((heads, RANK, HD), F32),
            pltpu.VMEM((2, heads, HD, HD), F32),
        ],
        compiler_params=pltpu.CompilerParams(vmem_limit_bytes=8 << 20),
        cost_estimate=pl.CostEstimate(flops=40_000_000, bytes_accessed=400_000, transcendentals=0),
    )(gram, start)


def attend(q, keys, vals, bias):
    row = lax.broadcasted_iota(jnp.int32, (QB, QB), 0)
    col = lax.broadcasted_iota(jnp.int32, (QB, QB), 1)
    old = col > row
    scores = [jnp.where(old, nt(q, keys[0]) + bias[0], nt(q, keys[4]))]
    scores += [nt(q, keys[b]) for b in (1, 2, 3)]
    peak = jnp.maximum(scores[0][:, :128], scores[0][:, 128:])
    for b in (1, 2, 3):
        peak = jnp.maximum(peak, jnp.maximum(scores[b][:, :128], scores[b][:, 128:]) + bias[b])
    peak = jnp.max(peak, axis=1, keepdims=True)
    edge = jnp.exp2((scores[0] - peak) * EXP2_SCALE)
    total = nn(jnp.where(old, edge, 0.0).astype(BF16), vals[0])
    total += nn(jnp.where(old, 0.0, edge).astype(BF16), vals[4])
    for b in (1, 2, 3):
        total += nn(jnp.exp2((scores[b] - (peak - bias[b])) * EXP2_SCALE).astype(BF16), vals[b])
    return total[:, :HD] / total[:, HD:]


def window_blocks(at_ref, k_ref, v_ref, near_ref, far_ref):
    first_valid = 4 - 2 * at_ref[0]
    ones = jnp.ones((QB, HD), BF16)
    keys, vals, bias = [], [], []
    for w in range(6):
        at = slice(w % 2 * QB, w % 2 * QB + QB)
        if w < 4:
            source = (far_ref, near_ref)[w // 2]
            key, val = source[0, at, :], source[1, at, :]
        else:
            key, val = k_ref[at, :], v_ref[at, :]
        keys.append(key)
        vals.append(jnp.concatenate([val, ones], axis=1))
        bias.append(jnp.where(w < first_valid, -BIG, 0.0).astype(F32))
    return keys, vals, bias


def attention_kernel(at_ref, q_ref, k_ref, v_ref, near_ref, far_ref, basis_ref, low_ref, mine_ref, theirs_ref):
    keys, vals, bias = window_blocks(at_ref, k_ref, v_ref, near_ref, far_ref)
    basis = basis_ref[0]
    low_keys = [nn(key, basis).astype(BF16) for key in keys]
    for qb in range(TOK // QB):
        rows = slice(qb * QB, (qb + 1) * QB)
        span = slice(qb, qb + 5)
        for j in range(2):
            cols = slice(j * HD, (j + 1) * HD)
            q = q_ref[rows, cols]
            exact = attend(q, keys[span], vals[span], bias[qb:])
            approx = attend(nn(q, basis).astype(BF16), low_keys[span], vals[span], bias[qb:])
            low_ref[rows, cols] = approx.astype(BF16)
            gap = (exact - approx).astype(BF16)
            for i in range(QB // (2 * CHUNK)):
                first = gap[2 * i * CHUNK : (2 * i + 1) * CHUNK]
                second = gap[(2 * i + 1) * CHUNK : (2 * i + 2) * CHUNK]
                to = slice(qb * QB // 2 + i * CHUNK, qb * QB // 2 + (i + 1) * CHUNK)
                mine_ref[to, cols] = jnp.where(at_ref[1] == 0, first, second)
                theirs_ref[to, cols] = jnp.where(at_ref[1] == 0, second, first)


def attention(at, queries, keys, values, near, far, basis):
    heads = basis.shape[0]
    pair = pl.BlockSpec((TOK, 2 * HD), lambda h, at: (0, h))
    one = pl.BlockSpec((TOK, HD), lambda h, at: (0, h))
    both = pl.BlockSpec((2, TOK, HD), lambda h, at: (0, 0, h))
    half = pl.BlockSpec((TOK // 2, 2 * HD), lambda h, at: (0, h))
    low = jax.ShapeDtypeStruct(queries.shape, BF16)
    gap = jax.ShapeDtypeStruct((TOK // 2, queries.shape[1]), BF16)
    return pl.pallas_call(
        attention_kernel,
        name="attention",
        out_shape=[low, gap, gap],
        grid_spec=pltpu.PrefetchScalarGridSpec(
            num_scalar_prefetch=1,
            grid=(heads,),
            in_specs=[pair, one, one, both, both, pl.BlockSpec((1, HD, RANK), lambda h, at: (h, 0, 0))],
            out_specs=[pair, half, half],
        ),
        compiler_params=pltpu.CompilerParams(vmem_limit_bytes=32 << 20),
        cost_estimate=pl.CostEstimate(
            flops=8 * TOK * 1280 * 512, bytes_accessed=6 << 20, transcendentals=8 * TOK * 1024
        ),
    )(at, queries, keys, values, near, far, basis)


def shards(queries, keys, values, start_basis, out_weight):
    z, y, core = (lax.axis_index(name).astype(jnp.int32) for name in ("z", "y", "core"))
    seq = NZ * NY
    swap = [(0, 1), (1, 0)]
    other_weight = lax.ppermute(out_weight, "core", swap)

    key_heads = keys.reshape(TOK, -1, HD)
    gram = jnp.einsum("thc,thd->hcd", key_heads, key_heads, preferred_element_type=F32)
    shape = gram.shape
    gram = lax.all_to_all(gram.reshape(seq, -1, HD), ("z", "y"), 0, 0, tiled=True).sum(0)
    paired = jnp.stack([keys, values])
    gram, paired = lax.optimization_barrier((gram, paired))
    passed = lax.ppermute(paired, "y", [(i, (i - 1) % NY) for i in range(NY)])
    gram = jnp.broadcast_to(gram[None], (seq,) + gram.shape)
    gram = lax.all_to_all(gram, ("z", "y"), 0, 0, tiled=True).reshape(shape)
    gram, paired, passed = lax.optimization_barrier((gram, paired, passed))

    near = lax.ppermute(paired, ("z", "y"), [(i, i + 1) for i in range(seq - 1)])
    holder = lambda i: i - 1 if i % NY else i + NY - 1
    far = lax.ppermute(passed, ("z", "y"), [(holder(i), i + 2) for i in range(seq - 2)])
    basis_half = find_basis(gram, start_basis.swapaxes(1, 2))

    at = jnp.stack([z * NY + y, core])
    in_place = lambda array: pltpu.with_memory_space_constraint(array, pltpu.HBM)
    lowrank_attn, mine, theirs = attention(at, *map(in_place, (queries, keys, values)), near, far, basis_half)

    theirs = lax.ppermute(theirs, "core", swap)
    partial = jnp.dot(mine, out_weight, preferred_element_type=F32)
    partial += jnp.dot(theirs, other_weight, preferred_element_type=F32)
    partial = partial.astype(BF16).reshape(NX, CHUNK, -1)
    partial = lax.all_to_all(partial, "x", 0, 0, tiled=True)
    return lowrank_attn, partial.astype(F32).sum(0).astype(BF16)


def solution(mesh):
    fine = Mesh(mesh.devices.reshape(NZ, NY, NX, 2), ("z", "y", "x", "core"))
    seq, head = ("z", "y"), ("x", "core")
    placed = (P(seq, head), P(seq, head), P(seq, head), P(head, None, None), P(head, None))
    return jax.shard_map(
        shards,
        mesh=fine,
        in_specs=placed,
        out_specs=(P(seq, head), P(seq + head, None)),
        check_vma=False,
    )
```

```python
import jax
import jax.numpy as jnp
from jax import lax
from jax.experimental import pallas as pl
from jax.experimental.pallas import tpu as pltpu
from jax.sharding import Mesh
from jax.sharding import PartitionSpec as P

HD = 128
QSCALE = 168
RANK = 64
TOK = 512
QB = 256
NZ, NY, NX = 16, 4, 4
CHUNK = TOK // (2 * NX)

HIGHEST = lax.Precision.HIGHEST
EXP2_SCALE = QSCALE**-0.5 * 1.4426950408889634
BIG = 1e30
F32, BF16 = jnp.float32, jnp.bfloat16

PLAN = (1, 1, 2, 2, 2)


def nt(a, b, precision=None):
    return lax.dot_general(a, b, (((1,), (1,)), ((), ())), precision=precision, preferred_element_type=F32)


def nn(a, b, precision=None):
    return lax.dot_general(a, b, (((1,), (0,)), ((), ())), precision=precision, preferred_element_type=F32)


def orthonormal_rows(rows_list):
    nb = 8
    groups = RANK // nb
    lane_shape = (nb, 2 * RANK)
    sub = lax.broadcasted_iota(jnp.int32, lane_shape, 0)
    eye = (
        lax.broadcasted_iota(jnp.int32, (RANK, RANK), 0)
        == lax.broadcasted_iota(jnp.int32, (RANK, RANK), 1)
    ).astype(F32)
    tables = []
    for z in rows_list:
        both = jnp.concatenate([nt(z, z, HIGHEST), eye], axis=1)
        tables.append([both[nb * g : nb * g + nb] for g in range(groups)])
    for g0 in range(groups):
        k0 = nb * g0
        for table in tables:
            rows = [jnp.broadcast_to(table[g0][j : j + 1, :], lane_shape) for j in range(nb)]
            cols = [
                [jnp.broadcast_to(table[g][:, k0 + j : k0 + j + 1], lane_shape) for g in range(g0, groups)]
                for j in range(nb)
            ]
            inner = [
                [jnp.broadcast_to(cols[j][0][i : i + 1, :], lane_shape) if j >= i else None for j in range(nb)]
                for i in range(nb)
            ]
            pivots = []
            for j in range(nb):
                inv = lax.rsqrt(inner[j][j])
                row = rows[j] * inv
                col = [c * inv for c in cols[j]]
                pivots.append((row, col))
                factors = [inner[j][k] * inv if k >= j else None for k in range(nb)]
                for k in range(j + 1, nb):
                    rows[k] = rows[k] - factors[k] * row
                    cols[k] = [a - b * factors[k] for a, b in zip(cols[k], col)]
                    for m in range(k, nb):
                        inner[k][m] = inner[k][m] - factors[k] * factors[m]
            for at, g in enumerate(range(g0, groups)):
                x = table[g]
                for j, (row, col) in enumerate(pivots):
                    less = x - col[at] * row
                    x = jnp.where(sub > j, less, jnp.where(sub == j, row, x)) if g == g0 else less
                table[g] = x
    return [
        nn(jnp.concatenate(table, axis=0)[:, RANK:], z, HIGHEST) for table, z in zip(tables, rows_list)
    ]


def basis_kernel(gram_ref, start_ref, out_ref, rows_ref, powers_ref):
    heads = start_ref.shape[0]
    grams = [gram_ref[h] for h in range(heads)]
    for h in range(heads):
        powers_ref[0, h] = grams[h]
        powers_ref[1, h] = nn(grams[h], grams[h], HIGHEST)
        rows_ref[h] = start_ref[h]
    singles = sum(1 for p in PLAN if p == 1)

    def step(i, carry):
        power = (i >= singles).astype(jnp.int32)
        moved = [nn(rows_ref[h], powers_ref[power, h], HIGHEST) for h in range(heads)]
        for h, rows in enumerate(orthonormal_rows(moved)):
            rows_ref[h] = rows
        return carry

    lax.fori_loop(0, len(PLAN), step, 0)
    for h in range(heads):
        out_ref[h] = rows_ref[h].T.astype(BF16)


def find_basis(gram, start):
    heads = start.shape[0]
    return pl.pallas_call(
        basis_kernel,
        name="basis",
        out_shape=jax.ShapeDtypeStruct((heads, HD, RANK), BF16),
        scratch_shapes=[
            pltpu.VMEM((heads, RANK, HD), F32),
            pltpu.VMEM((2, heads, HD, HD), F32),
        ],
        compiler_params=pltpu.CompilerParams(vmem_limit_bytes=8 << 20),
        cost_estimate=pl.CostEstimate(flops=40_000_000, bytes_accessed=400_000, transcendentals=0),
    )(gram, start)


def attend(q, keys, vals, bias):
    row = lax.broadcasted_iota(jnp.int32, (QB, QB), 0)
    col = lax.broadcasted_iota(jnp.int32, (QB, QB), 1)
    old = col > row
    scores = [jnp.where(old, nt(q, keys[0]) + bias[0], nt(q, keys[4]))]
    scores += [nt(q, keys[b]) for b in (1, 2, 3)]
    peak = jnp.maximum(scores[0][:, :128], scores[0][:, 128:])
    for b in (1, 2, 3):
        peak = jnp.maximum(peak, jnp.maximum(scores[b][:, :128], scores[b][:, 128:]) + bias[b])
    peak = jnp.max(peak, axis=1, keepdims=True)
    edge = jnp.exp2((scores[0] - peak) * EXP2_SCALE)
    total = nn(jnp.where(old, edge, 0.0).astype(BF16), vals[0])
    total += nn(jnp.where(old, 0.0, edge).astype(BF16), vals[4])
    for b in (1, 2, 3):
        total += nn(jnp.exp2((scores[b] - (peak - bias[b])) * EXP2_SCALE).astype(BF16), vals[b])
    return total[:, :HD] / total[:, HD:]


def window_blocks(at_ref, k_ref, v_ref, near_ref, far_ref):
    first_valid = 4 - 2 * at_ref[0]
    ones = jnp.ones((QB, HD), BF16)
    keys, vals, bias = [], [], []
    for w in range(6):
        at = slice(w % 2 * QB, w % 2 * QB + QB)
        if w < 4:
            source = (far_ref, near_ref)[w // 2]
            key, val = source[0, at, :], source[1, at, :]
        else:
            key, val = k_ref[at, :], v_ref[at, :]
        keys.append(key)
        vals.append(jnp.concatenate([val, ones], axis=1))
        bias.append(jnp.where(w < first_valid, -BIG, 0.0).astype(F32))
    return keys, vals, bias


def tiles():
    for qb in range(TOK // QB):
        for j in range(2):
            yield qb, slice(qb * QB, (qb + 1) * QB), slice(j * HD, (j + 1) * HD)


def exact_kernel(at_ref, q_ref, k_ref, v_ref, near_ref, far_ref, out_ref):
    keys, vals, bias = window_blocks(at_ref, k_ref, v_ref, near_ref, far_ref)
    for qb, rows, cols in tiles():
        out_ref[rows, cols] = attend(q_ref[rows, cols], keys[qb : qb + 5], vals[qb : qb + 5], bias[qb:])


def approx_kernel(
    at_ref, q_ref, k_ref, v_ref, near_ref, far_ref, basis_ref, exact_ref, low_ref, mine_ref, theirs_ref
):
    keys, vals, bias = window_blocks(at_ref, k_ref, v_ref, near_ref, far_ref)
    basis = basis_ref[0]
    keys = [nn(key, basis).astype(BF16) for key in keys]
    for qb, rows, cols in tiles():
        q = nn(q_ref[rows, cols], basis).astype(BF16)
        approx = attend(q, keys[qb : qb + 5], vals[qb : qb + 5], bias[qb:])
        low_ref[rows, cols] = approx.astype(BF16)
        gap = (exact_ref[rows, cols] - approx).astype(BF16)
        for i in range(QB // (2 * CHUNK)):
            first = gap[2 * i * CHUNK : (2 * i + 1) * CHUNK]
            second = gap[(2 * i + 1) * CHUNK : (2 * i + 2) * CHUNK]
            to = slice(qb * QB // 2 + i * CHUNK, qb * QB // 2 + (i + 1) * CHUNK)
            mine_ref[to, cols] = jnp.where(at_ref[1] == 0, first, second)
            theirs_ref[to, cols] = jnp.where(at_ref[1] == 0, second, first)


PAIR = pl.BlockSpec((TOK, 2 * HD), lambda h, at: (0, h))
ONE = pl.BlockSpec((TOK, HD), lambda h, at: (0, h))
BOTH = pl.BlockSpec((2, TOK, HD), lambda h, at: (0, 0, h))
HALF = pl.BlockSpec((TOK // 2, 2 * HD), lambda h, at: (0, h))
BASIS = pl.BlockSpec((1, HD, RANK), lambda h, at: (h, 0, 0))
WINDOW = [PAIR, ONE, ONE, BOTH, BOTH]


def attention(kernel, name, in_specs, out_specs, out_shape, operands):
    return pl.pallas_call(
        kernel,
        name=name,
        out_shape=out_shape,
        grid_spec=pltpu.PrefetchScalarGridSpec(
            num_scalar_prefetch=1,
            grid=(operands[2].shape[1] // HD,),
            in_specs=in_specs,
            out_specs=out_specs,
        ),
        compiler_params=pltpu.CompilerParams(vmem_limit_bytes=20 << 20),
        cost_estimate=pl.CostEstimate(
            flops=4 * TOK * 1280 * 512, bytes_accessed=4 << 20, transcendentals=4 * TOK * 1024
        ),
    )(*operands)


def shards(queries, keys, values, start_basis, out_weight):
    z, y, core = (lax.axis_index(name).astype(jnp.int32) for name in ("z", "y", "core"))
    seq = NZ * NY
    swap = [(0, 1), (1, 0)]
    in_place = lambda array: pltpu.with_memory_space_constraint(array, pltpu.HBM)
    held = (jnp.stack([z * NY + y, core]), *map(in_place, (queries, keys, values)))

    key_heads = keys.reshape(TOK, -1, HD)
    gram = jnp.einsum("thc,thd->hcd", key_heads, key_heads, preferred_element_type=F32)
    shape = gram.shape
    gram, keys, values = lax.optimization_barrier((gram, keys, values))
    gram = lax.all_to_all(gram.reshape(seq, -1, HD), ("z", "y"), 0, 0, tiled=True).sum(0)
    paired = jnp.stack([keys, values])
    near = lax.ppermute(paired, ("z", "y"), [(i, i + 1) for i in range(seq - 1)])
    passed = lax.ppermute(paired, "y", [(i, (i - 1) % NY) for i in range(NY)])
    gram, passed, out_weight = lax.optimization_barrier((gram, passed, out_weight))
    other_weight = lax.ppermute(out_weight, "core", swap)
    holder = lambda i: i - 1 if i % NY else i + NY - 1
    far = lax.ppermute(passed, ("z", "y"), [(holder(i), i + 2) for i in range(seq - 2)])
    gram = jnp.broadcast_to(gram[None], (seq,) + gram.shape)
    gram = lax.all_to_all(gram, ("z", "y"), 0, 0, tiled=True).reshape(shape)
    exact = attention(
        exact_kernel,
        "exact",
        WINDOW,
        PAIR,
        jax.ShapeDtypeStruct(queries.shape, F32),
        held + (near, far),
    )
    gram, exact = lax.optimization_barrier((gram, exact))
    basis_half = find_basis(gram, start_basis.swapaxes(1, 2))

    low = jax.ShapeDtypeStruct(queries.shape, BF16)
    half = jax.ShapeDtypeStruct((TOK // 2, queries.shape[1]), BF16)
    lowrank_attn, mine, theirs = attention(
        approx_kernel,
        "approx",
        WINDOW + [BASIS, PAIR],
        [PAIR, HALF, HALF],
        [low, half, half],
        held + (in_place(near), in_place(far), basis_half, exact),
    )

    theirs = lax.ppermute(theirs, "core", swap)
    partial = jnp.dot(mine, out_weight, preferred_element_type=F32)
    partial += jnp.dot(theirs, other_weight, preferred_element_type=F32)
    partial = partial.astype(BF16).reshape(NX, CHUNK, -1)
    partial = lax.all_to_all(partial, "x", 0, 0, tiled=True)
    return lowrank_attn, partial.astype(F32).sum(0).astype(BF16)


def solution(mesh):
    fine = Mesh(mesh.devices.reshape(NZ, NY, NX, 2), ("z", "y", "x", "core"))
    seq, head = ("z", "y"), ("x", "core")
    placed = (P(seq, head), P(seq, head), P(seq, head), P(head, None, None), P(head, None))
    return jax.shard_map(
        shards,
        mesh=fine,
        in_specs=placed,
        out_specs=(P(seq, head), P(seq + head, None)),
        check_vma=False,
    )
```

```python
import jax
import jax.numpy as jnp
from jax import lax
from jax.experimental import pallas as pl
from jax.experimental.pallas import tpu as pltpu
from jax.sharding import Mesh
from jax.sharding import PartitionSpec as P

HD = 128
QSCALE = 168
RANK = 64
TOK = 512
QB = 256
NZ, NY, NX = 16, 4, 4
CHUNK = TOK // (2 * NX)

HIGHEST = lax.Precision.HIGHEST
EXP2_SCALE = QSCALE**-0.5 * 1.4426950408889634
BIG = 1e30
F32, BF16 = jnp.float32, jnp.bfloat16

PLAN = (1, 1, 2, 2, 2)


def nt(a, b, precision=None):
    return lax.dot_general(a, b, (((1,), (1,)), ((), ())), precision=precision, preferred_element_type=F32)


def nn(a, b, precision=None):
    return lax.dot_general(a, b, (((1,), (0,)), ((), ())), precision=precision, preferred_element_type=F32)


def orthonormal_rows(rows_list):
    nb = 8
    groups = RANK // nb
    lane_shape = (nb, 2 * RANK)
    sub = lax.broadcasted_iota(jnp.int32, lane_shape, 0)
    eye = (
        lax.broadcasted_iota(jnp.int32, (RANK, RANK), 0)
        == lax.broadcasted_iota(jnp.int32, (RANK, RANK), 1)
    ).astype(F32)
    tables = []
    for z in rows_list:
        both = jnp.concatenate([nt(z, z, HIGHEST), eye], axis=1)
        tables.append([both[nb * g : nb * g + nb] for g in range(groups)])
    for g0 in range(groups):
        k0 = nb * g0
        for table in tables:
            rows = [jnp.broadcast_to(table[g0][j : j + 1, :], lane_shape) for j in range(nb)]
            cols = [
                [jnp.broadcast_to(table[g][:, k0 + j : k0 + j + 1], lane_shape) for g in range(g0, groups)]
                for j in range(nb)
            ]
            inner = [
                [jnp.broadcast_to(cols[j][0][i : i + 1, :], lane_shape) if j >= i else None for j in range(nb)]
                for i in range(nb)
            ]
            pivots = []
            for j in range(nb):
                inv = lax.rsqrt(inner[j][j])
                row = rows[j] * inv
                col = [c * inv for c in cols[j]]
                pivots.append((row, col))
                factors = [inner[j][k] * inv if k >= j else None for k in range(nb)]
                for k in range(j + 1, nb):
                    rows[k] = rows[k] - factors[k] * row
                    cols[k] = [a - b * factors[k] for a, b in zip(cols[k], col)]
                    for m in range(k, nb):
                        inner[k][m] = inner[k][m] - factors[k] * factors[m]
            for at, g in enumerate(range(g0, groups)):
                x = table[g]
                for j, (row, col) in enumerate(pivots):
                    less = x - col[at] * row
                    x = jnp.where(sub > j, less, jnp.where(sub == j, row, x)) if g == g0 else less
                table[g] = x
    return [
        nn(jnp.concatenate(table, axis=0)[:, RANK:], z, HIGHEST) for table, z in zip(tables, rows_list)
    ]


def basis_kernel(gram_ref, start_ref, out_ref, rows_ref, powers_ref):
    heads = start_ref.shape[0]
    grams = [gram_ref[h] for h in range(heads)]
    for h in range(heads):
        powers_ref[0, h] = grams[h]
        powers_ref[1, h] = nn(grams[h], grams[h], HIGHEST)
        rows_ref[h] = start_ref[h]
    singles = sum(1 for p in PLAN if p == 1)

    def step(i, carry):
        power = (i >= singles).astype(jnp.int32)
        moved = [nn(rows_ref[h], powers_ref[power, h], HIGHEST) for h in range(heads)]
        for h, rows in enumerate(orthonormal_rows(moved)):
            rows_ref[h] = rows
        return carry

    lax.fori_loop(0, len(PLAN), step, 0)
    for h in range(heads):
        out_ref[h] = rows_ref[h].T.astype(BF16)


def find_basis(gram, start):
    heads = start.shape[0]
    return pl.pallas_call(
        basis_kernel,
        name="basis",
        out_shape=jax.ShapeDtypeStruct((heads, HD, RANK), BF16),
        scratch_shapes=[
            pltpu.VMEM((heads, RANK, HD), F32),
            pltpu.VMEM((2, heads, HD, HD), F32),
        ],
        compiler_params=pltpu.CompilerParams(vmem_limit_bytes=8 << 20),
        cost_estimate=pl.CostEstimate(flops=40_000_000, bytes_accessed=400_000, transcendentals=0),
    )(gram, start)


def attend(q, keys, vals, bias):
    row = lax.broadcasted_iota(jnp.int32, (QB, QB), 0)
    col = lax.broadcasted_iota(jnp.int32, (QB, QB), 1)
    old = col > row
    scores = [jnp.where(old, nt(q, keys[0]) + bias[0], nt(q, keys[4]))]
    scores += [nt(q, keys[b]) for b in (1, 2, 3)]
    peak = jnp.maximum(scores[0][:, :128], scores[0][:, 128:])
    for b in (1, 2, 3):
        peak = jnp.maximum(peak, jnp.maximum(scores[b][:, :128], scores[b][:, 128:]) + bias[b])
    peak = jnp.max(peak, axis=1, keepdims=True)
    edge = jnp.exp2((scores[0] - peak) * EXP2_SCALE)
    total = nn(jnp.where(old, edge, 0.0).astype(BF16), vals[0])
    total += nn(jnp.where(old, 0.0, edge).astype(BF16), vals[4])
    for b in (1, 2, 3):
        total += nn(jnp.exp2((scores[b] - (peak - bias[b])) * EXP2_SCALE).astype(BF16), vals[b])
    return total[:, :HD] / total[:, HD:]


def window_blocks(at_ref, k_ref, v_ref, near_ref, far_ref):
    first_valid = 4 - 2 * at_ref[0]
    ones = jnp.ones((QB, HD), BF16)
    keys, vals, bias = [], [], []
    for w in range(6):
        at = slice(w % 2 * QB, w % 2 * QB + QB)
        if w < 4:
            source = (far_ref, near_ref)[w // 2]
            key, val = source[0, at, :], source[1, at, :]
        else:
            key, val = k_ref[at, :], v_ref[at, :]
        keys.append(key)
        vals.append(jnp.concatenate([val, ones], axis=1))
        bias.append(jnp.where(w < first_valid, -BIG, 0.0).astype(F32))
    return keys, vals, bias


def tiles():
    for qb in range(TOK // QB):
        for j in range(2):
            yield qb, slice(qb * QB, (qb + 1) * QB), slice(j * HD, (j + 1) * HD)


def exact_kernel(at_ref, q_ref, k_ref, v_ref, near_ref, far_ref, out_ref):
    keys, vals, bias = window_blocks(at_ref, k_ref, v_ref, near_ref, far_ref)
    for qb, rows, cols in tiles():
        out_ref[rows, cols] = attend(q_ref[rows, cols], keys[qb : qb + 5], vals[qb : qb + 5], bias[qb:])


def approx_kernel(
    at_ref, q_ref, k_ref, v_ref, near_ref, far_ref, basis_ref, exact_ref, low_ref, mine_ref, theirs_ref
):
    keys, vals, bias = window_blocks(at_ref, k_ref, v_ref, near_ref, far_ref)
    basis = basis_ref[0]
    keys = [nn(key, basis).astype(BF16) for key in keys]
    for qb, rows, cols in tiles():
        q = nn(q_ref[rows, cols], basis).astype(BF16)
        approx = attend(q, keys[qb : qb + 5], vals[qb : qb + 5], bias[qb:])
        low_ref[rows, cols] = approx.astype(BF16)
        gap = (exact_ref[rows, cols] - approx).astype(BF16)
        for i in range(QB // (2 * CHUNK)):
            first = gap[2 * i * CHUNK : (2 * i + 1) * CHUNK]
            second = gap[(2 * i + 1) * CHUNK : (2 * i + 2) * CHUNK]
            to = slice(qb * QB // 2 + i * CHUNK, qb * QB // 2 + (i + 1) * CHUNK)
            mine_ref[to, cols] = jnp.where(at_ref[1] == 0, first, second)
            theirs_ref[to, cols] = jnp.where(at_ref[1] == 0, second, first)


PAIR = pl.BlockSpec((TOK, 2 * HD), lambda h, at: (0, h))
ONE = pl.BlockSpec((TOK, HD), lambda h, at: (0, h))
BOTH = pl.BlockSpec((2, TOK, HD), lambda h, at: (0, 0, h))
HALF = pl.BlockSpec((TOK // 2, 2 * HD), lambda h, at: (0, h))
BASIS = pl.BlockSpec((1, HD, RANK), lambda h, at: (h, 0, 0))
WINDOW = [PAIR, ONE, ONE, BOTH, BOTH]


def attention(kernel, name, in_specs, out_specs, out_shape, operands):
    return pl.pallas_call(
        kernel,
        name=name,
        out_shape=out_shape,
        grid_spec=pltpu.PrefetchScalarGridSpec(
            num_scalar_prefetch=1,
            grid=(operands[2].shape[1] // HD,),
            in_specs=in_specs,
            out_specs=out_specs,
        ),
        compiler_params=pltpu.CompilerParams(vmem_limit_bytes=20 << 20),
        cost_estimate=pl.CostEstimate(
            flops=4 * TOK * 1280 * 512, bytes_accessed=4 << 20, transcendentals=4 * TOK * 1024
        ),
    )(*operands)


def project_kernel(mine_ref, theirs_ref, own_ref, other_ref, out_ref):
    total = nn(mine_ref[...], own_ref[...]) + nn(theirs_ref[...], other_ref[...])
    out_ref[...] = total.astype(BF16)


def project(mine, theirs, own, other):
    rows, feats = mine.shape
    width = own.shape[1]
    step = width // 3
    left = pl.BlockSpec((rows, feats), lambda n: (0, 0))
    right = pl.BlockSpec((feats, step), lambda n: (0, n))
    return pl.pallas_call(
        project_kernel,
        name="project",
        out_shape=jax.ShapeDtypeStruct((rows, width), BF16),
        grid=(width // step,),
        in_specs=[left, left, right, right],
        out_specs=pl.BlockSpec((rows, step), lambda n: (0, n)),
        compiler_params=pltpu.CompilerParams(vmem_limit_bytes=16 << 20),
        cost_estimate=pl.CostEstimate(
            flops=4 * rows * feats * width, bytes_accessed=4 * feats * width, transcendentals=0
        ),
    )(mine, theirs, own, other)


def shards(queries, keys, values, start_basis, out_weight):
    z, y, core = (lax.axis_index(name).astype(jnp.int32) for name in ("z", "y", "core"))
    seq = NZ * NY
    swap = [(0, 1), (1, 0)]
    in_place = lambda array: pltpu.with_memory_space_constraint(array, pltpu.HBM)
    held = (jnp.stack([z * NY + y, core]), *map(in_place, (queries, keys, values)))

    key_heads = keys.reshape(TOK, -1, HD)
    gram = jnp.einsum("thc,thd->hcd", key_heads, key_heads, preferred_element_type=F32)
    shape = gram.shape
    gram, keys, values = lax.optimization_barrier((gram, keys, values))
    gram = lax.all_to_all(gram.reshape(seq, -1, HD), ("z", "y"), 0, 0, tiled=True).sum(0)
    paired = jnp.stack([keys, values])
    near = lax.ppermute(paired, ("z", "y"), [(i, i + 1) for i in range(seq - 1)])
    passed = lax.ppermute(paired, "y", [(i, (i - 1) % NY) for i in range(NY)])
    holder = lambda i: i - 1 if i % NY else i + NY - 1
    far = lax.ppermute(passed, ("z", "y"), [(holder(i), i + 2) for i in range(seq - 2)])
    other_weight = lax.ppermute(out_weight, "core", swap)
    gram = jnp.broadcast_to(gram[None], (seq,) + gram.shape)
    gram = lax.all_to_all(gram, ("z", "y"), 0, 0, tiled=True).reshape(shape)
    exact = attention(
        exact_kernel,
        "exact",
        WINDOW,
        PAIR,
        jax.ShapeDtypeStruct(queries.shape, F32),
        held + (near, far),
    )
    gram, exact = lax.optimization_barrier((gram, exact))
    basis_half = find_basis(gram, start_basis.swapaxes(1, 2))

    low = jax.ShapeDtypeStruct(queries.shape, BF16)
    half = jax.ShapeDtypeStruct((TOK // 2, queries.shape[1]), BF16)
    lowrank_attn, mine, theirs = attention(
        approx_kernel,
        "approx",
        WINDOW + [BASIS, PAIR],
        [PAIR, HALF, HALF],
        [low, half, half],
        held + (in_place(near), in_place(far), basis_half, exact),
    )

    theirs = lax.ppermute(theirs, "core", swap)
    partial = project(mine, theirs, in_place(out_weight), in_place(other_weight)).reshape(NX, CHUNK, -1)
    partial = lax.all_to_all(partial, "x", 0, 0, tiled=True)
    return lowrank_attn, partial.astype(F32).sum(0).astype(BF16)


def solution(mesh):
    fine = Mesh(mesh.devices.reshape(NZ, NY, NX, 2), ("z", "y", "x", "core"))
    seq, head = ("z", "y"), ("x", "core")
    placed = (P(seq, head), P(seq, head), P(seq, head), P(head, None, None), P(head, None))
    return jax.shard_map(
        shards,
        mesh=fine,
        in_specs=placed,
        out_specs=(P(seq, head), P(seq + head, None)),
        check_vma=False,
    )
```

```python
import jax
import jax.numpy as jnp
from jax import lax
from jax.experimental import pallas as pl
from jax.experimental.pallas import tpu as pltpu
from jax.sharding import Mesh
from jax.sharding import PartitionSpec as P

HD = 128
QSCALE = 168
RANK = 64
TOK = 512
QB = 256
NZ, NY, NX = 16, 4, 4
CHUNK = TOK // (2 * NX)

HIGHEST = lax.Precision.HIGHEST
EXP2_SCALE = QSCALE**-0.5 * 1.4426950408889634
BIG = 1e30
F32, BF16 = jnp.float32, jnp.bfloat16

PLAN = (1, 1, 2, 2, 2)


def nt(a, b, precision=None):
    return lax.dot_general(a, b, (((1,), (1,)), ((), ())), precision=precision, preferred_element_type=F32)


def nn(a, b, precision=None):
    return lax.dot_general(a, b, (((1,), (0,)), ((), ())), precision=precision, preferred_element_type=F32)


def orthonormal_rows(rows_list):
    nb = 8
    groups = RANK // nb
    lane_shape = (nb, 2 * RANK)
    sub = lax.broadcasted_iota(jnp.int32, lane_shape, 0)
    eye = (
        lax.broadcasted_iota(jnp.int32, (RANK, RANK), 0)
        == lax.broadcasted_iota(jnp.int32, (RANK, RANK), 1)
    ).astype(F32)
    tables = []
    for z in rows_list:
        both = jnp.concatenate([nt(z, z, HIGHEST), eye], axis=1)
        tables.append([both[nb * g : nb * g + nb] for g in range(groups)])
    for g0 in range(groups):
        k0 = nb * g0
        for table in tables:
            rows = [jnp.broadcast_to(table[g0][j : j + 1, :], lane_shape) for j in range(nb)]
            cols = [
                [jnp.broadcast_to(table[g][:, k0 + j : k0 + j + 1], lane_shape) for g in range(g0, groups)]
                for j in range(nb)
            ]
            inner = [
                [jnp.broadcast_to(cols[j][0][i : i + 1, :], lane_shape) if j >= i else None for j in range(nb)]
                for i in range(nb)
            ]
            pivots = []
            for j in range(nb):
                inv = lax.rsqrt(inner[j][j])
                row = rows[j] * inv
                col = [c * inv for c in cols[j]]
                pivots.append((row, col))
                factors = [inner[j][k] * inv if k >= j else None for k in range(nb)]
                for k in range(j + 1, nb):
                    rows[k] = rows[k] - factors[k] * row
                    cols[k] = [a - b * factors[k] for a, b in zip(cols[k], col)]
                    for m in range(k, nb):
                        inner[k][m] = inner[k][m] - factors[k] * factors[m]
            for at, g in enumerate(range(g0, groups)):
                x = table[g]
                for j, (row, col) in enumerate(pivots):
                    less = x - col[at] * row
                    x = jnp.where(sub > j, less, jnp.where(sub == j, row, x)) if g == g0 else less
                table[g] = x
    return [
        nn(jnp.concatenate(table, axis=0)[:, RANK:], z, HIGHEST) for table, z in zip(tables, rows_list)
    ]


def prepare_kernel(k_ref, v_ref, gram_ref, paired_ref):
    paired_ref[0] = k_ref[...]
    paired_ref[1] = v_ref[...]
    for h in range(gram_ref.shape[0]):
        k = k_ref[:, h * HD : (h + 1) * HD]
        gram_ref[h] = lax.dot_general(k, k, (((0,), (0,)), ((), ())), preferred_element_type=F32)


def prepare(keys, values):
    heads = keys.shape[1] // HD
    return pl.pallas_call(
        prepare_kernel,
        name="prepare",
        out_shape=[
            jax.ShapeDtypeStruct((heads, HD, HD), F32),
            jax.ShapeDtypeStruct((2,) + keys.shape, BF16),
        ],
        compiler_params=pltpu.CompilerParams(vmem_limit_bytes=8 << 20),
        cost_estimate=pl.CostEstimate(
            flops=2 * heads * TOK * HD * HD, bytes_accessed=8 * keys.size, transcendentals=0
        ),
    )(keys, values)


def basis_kernel(gram_ref, start_ref, out_ref, rows_ref, powers_ref):
    heads = start_ref.shape[0]
    grams = [gram_ref[h] for h in range(heads)]
    row = lax.broadcasted_iota(jnp.int32, (HD, HD), 0)
    col = lax.broadcasted_iota(jnp.int32, (HD, HD), 1)
    for h in range(heads):
        trace = jnp.sum(jnp.where(row == col, grams[h], 0.0))
        powers_ref[0, h] = grams[h]
        powers_ref[1, h] = nn(grams[h], grams[h] / trace, HIGHEST)
        rows_ref[h] = start_ref[h]
    singles = sum(1 for p in PLAN if p == 1)

    def step(i, carry):
        power = (i >= singles).astype(jnp.int32)
        moved = [nn(rows_ref[h], powers_ref[power, h], HIGHEST) for h in range(heads)]
        for h, rows in enumerate(orthonormal_rows(moved)):
            rows_ref[h] = rows
        return carry

    lax.fori_loop(0, len(PLAN), step, 0)
    for h in range(heads):
        out_ref[h] = rows_ref[h].T.astype(BF16)


def find_basis(gram, start):
    heads = start.shape[0]
    return pl.pallas_call(
        basis_kernel,
        name="basis",
        out_shape=jax.ShapeDtypeStruct((heads, HD, RANK), BF16),
        scratch_shapes=[
            pltpu.VMEM((heads, RANK, HD), F32),
            pltpu.VMEM((2, heads, HD, HD), F32),
        ],
        compiler_params=pltpu.CompilerParams(vmem_limit_bytes=8 << 20),
        cost_estimate=pl.CostEstimate(flops=40_000_000, bytes_accessed=400_000, transcendentals=0),
    )(gram, start)


def attend(q, keys, vals, bias):
    row = lax.broadcasted_iota(jnp.int32, (QB, QB), 0)
    col = lax.broadcasted_iota(jnp.int32, (QB, QB), 1)
    old = col > row
    scores = [jnp.where(old, nt(q, keys[0]) + bias[0], nt(q, keys[4]))]
    scores += [nt(q, keys[b]) for b in (1, 2, 3)]
    peak = jnp.maximum(scores[0][:, :128], scores[0][:, 128:])
    for b in (1, 2, 3):
        peak = jnp.maximum(peak, jnp.maximum(scores[b][:, :128], scores[b][:, 128:]) + bias[b])
    peak = jnp.max(peak, axis=1, keepdims=True)
    edge = jnp.exp2((scores[0] - peak) * EXP2_SCALE)
    total = nn(jnp.where(old, edge, 0.0).astype(BF16), vals[0])
    total += nn(jnp.where(old, 0.0, edge).astype(BF16), vals[4])
    for b in (1, 2, 3):
        total += nn(jnp.exp2((scores[b] - (peak - bias[b])) * EXP2_SCALE).astype(BF16), vals[b])
    return total[:, :HD] / total[:, HD:]


def window_blocks(at_ref, k_ref, v_ref, near_ref, far_ref):
    first_valid = 4 - 2 * at_ref[0]
    ones = jnp.ones((QB, HD), BF16)
    keys, vals, bias = [], [], []
    for w in range(6):
        at = slice(w % 2 * QB, w % 2 * QB + QB)
        if w < 4:
            source = (far_ref, near_ref)[w // 2]
            key, val = source[0, at, :], source[1, at, :]
        else:
            key, val = k_ref[at, :], v_ref[at, :]
        keys.append(key)
        vals.append(jnp.concatenate([val, ones], axis=1))
        bias.append(jnp.where(w < first_valid, -BIG, 0.0).astype(F32))
    return keys, vals, bias


def tiles():
    for qb in range(TOK // QB):
        for j in range(2):
            yield qb, slice(qb * QB, (qb + 1) * QB), slice(j * HD, (j + 1) * HD)


def exact_kernel(at_ref, q_ref, k_ref, v_ref, near_ref, far_ref, out_ref):
    keys, vals, bias = window_blocks(at_ref, k_ref, v_ref, near_ref, far_ref)
    for qb, rows, cols in tiles():
        out_ref[rows, cols] = attend(q_ref[rows, cols], keys[qb : qb + 5], vals[qb : qb + 5], bias[qb:])


def approx_kernel(
    at_ref, q_ref, k_ref, v_ref, near_ref, far_ref, basis_ref, exact_ref, low_ref, mine_ref, theirs_ref
):
    keys, vals, bias = window_blocks(at_ref, k_ref, v_ref, near_ref, far_ref)
    basis = basis_ref[0]
    keys = [nn(key, basis).astype(BF16) for key in keys]
    for qb, rows, cols in tiles():
        q = nn(q_ref[rows, cols], basis).astype(BF16)
        approx = attend(q, keys[qb : qb + 5], vals[qb : qb + 5], bias[qb:])
        low_ref[rows, cols] = approx.astype(BF16)
        gap = (exact_ref[rows, cols] - approx).astype(BF16)
        for i in range(QB // (2 * CHUNK)):
            first = gap[2 * i * CHUNK : (2 * i + 1) * CHUNK]
            second = gap[(2 * i + 1) * CHUNK : (2 * i + 2) * CHUNK]
            to = slice(qb * QB // 2 + i * CHUNK, qb * QB // 2 + (i + 1) * CHUNK)
            mine_ref[to, cols] = jnp.where(at_ref[1] == 0, first, second)
            theirs_ref[to, cols] = jnp.where(at_ref[1] == 0, second, first)


PAIR = pl.BlockSpec((TOK, 2 * HD), lambda h, at: (0, h))
ONE = pl.BlockSpec((TOK, HD), lambda h, at: (0, h))
BOTH = pl.BlockSpec((2, TOK, HD), lambda h, at: (0, 0, h))
HALF = pl.BlockSpec((TOK // 2, 2 * HD), lambda h, at: (0, h))
BASIS = pl.BlockSpec((1, HD, RANK), lambda h, at: (h, 0, 0))
WINDOW = [PAIR, ONE, ONE, BOTH, BOTH]


def attention(kernel, name, in_specs, out_specs, out_shape, operands):
    return pl.pallas_call(
        kernel,
        name=name,
        out_shape=out_shape,
        grid_spec=pltpu.PrefetchScalarGridSpec(
            num_scalar_prefetch=1,
            grid=(operands[2].shape[1] // HD,),
            in_specs=in_specs,
            out_specs=out_specs,
        ),
        compiler_params=pltpu.CompilerParams(vmem_limit_bytes=20 << 20),
        cost_estimate=pl.CostEstimate(
            flops=4 * TOK * 1280 * 512, bytes_accessed=4 << 20, transcendentals=4 * TOK * 1024
        ),
    )(*operands)


def project_kernel(mine_ref, theirs_ref, own_ref, other_ref, out_ref):
    total = nn(mine_ref[...], own_ref[...]) + nn(theirs_ref[...], other_ref[...])
    out_ref[...] = total.astype(BF16)


def project(mine, theirs, own, other):
    rows, feats = mine.shape
    width = own.shape[1]
    step = width // 3
    left = pl.BlockSpec((rows, feats), lambda n: (0, 0))
    right = pl.BlockSpec((feats, step), lambda n: (0, n))
    return pl.pallas_call(
        project_kernel,
        name="project",
        out_shape=jax.ShapeDtypeStruct((rows, width), BF16),
        grid=(width // step,),
        in_specs=[left, left, right, right],
        out_specs=pl.BlockSpec((rows, step), lambda n: (0, n)),
        compiler_params=pltpu.CompilerParams(vmem_limit_bytes=16 << 20),
        cost_estimate=pl.CostEstimate(
            flops=4 * rows * feats * width, bytes_accessed=4 * feats * width, transcendentals=0
        ),
    )(mine, theirs, own, other)


def shards(queries, keys, values, start_basis, out_weight):
    z, y, core = (lax.axis_index(name).astype(jnp.int32) for name in ("z", "y", "core"))
    seq = NZ * NY
    swap = [(0, 1), (1, 0)]
    in_place = lambda array: pltpu.with_memory_space_constraint(array, pltpu.HBM)
    held = (jnp.stack([z * NY + y, core]), *map(in_place, (queries, keys, values)))

    gram, paired = prepare(in_place(keys), in_place(values))
    shape = gram.shape
    gram = lax.all_to_all(gram.reshape(seq, -1, HD), ("z", "y"), 0, 0, tiled=True).sum(0)
    near = lax.ppermute(paired, ("z", "y"), [(i, i + 1) for i in range(seq - 1)])
    passed = lax.ppermute(paired, "y", [(i, (i - 1) % NY) for i in range(NY)])
    holder = lambda i: i - 1 if i % NY else i + NY - 1
    far = lax.ppermute(passed, ("z", "y"), [(holder(i), i + 2) for i in range(seq - 2)])
    other_weight = lax.ppermute(out_weight, "core", swap)
    gram = jnp.broadcast_to(gram[None], (seq,) + gram.shape)
    gram = lax.all_to_all(gram, ("z", "y"), 0, 0, tiled=True).reshape(shape)
    exact = attention(
        exact_kernel,
        "exact",
        WINDOW,
        PAIR,
        jax.ShapeDtypeStruct(queries.shape, F32),
        held + (near, far),
    )
    gram, exact = lax.optimization_barrier((gram, exact))
    basis_half = find_basis(gram, start_basis.swapaxes(1, 2))

    low = jax.ShapeDtypeStruct(queries.shape, BF16)
    half = jax.ShapeDtypeStruct((TOK // 2, queries.shape[1]), BF16)
    lowrank_attn, mine, theirs = attention(
        approx_kernel,
        "approx",
        WINDOW + [BASIS, PAIR],
        [PAIR, HALF, HALF],
        [low, half, half],
        held + (in_place(near), in_place(far), basis_half, in_place(exact)),
    )

    theirs = lax.ppermute(theirs, "core", swap)
    partial = project(mine, theirs, out_weight, other_weight).reshape(NX, CHUNK, -1)
    partial = lax.all_to_all(partial, "x", 0, 0, tiled=True)
    return lowrank_attn, partial.astype(F32).sum(0).astype(BF16)


def solution(mesh):
    fine = Mesh(mesh.devices.reshape(NZ, NY, NX, 2), ("z", "y", "x", "core"))
    seq, head = ("z", "y"), ("x", "core")
    placed = (P(seq, head), P(seq, head), P(seq, head), P(head, None, None), P(head, None))
    return jax.shard_map(
        shards,
        mesh=fine,
        in_specs=placed,
        out_specs=(P(seq, head), P(seq + head, None)),
        check_vma=False,
    )
```

```python
import jax
import jax.numpy as jnp
from jax import lax
from jax.experimental import pallas as pl
from jax.experimental.pallas import tpu as pltpu
from jax.sharding import Mesh
from jax.sharding import PartitionSpec as P

HD = 128
QSCALE = 168
RANK = 64
TOK = 512
QB = 256
NZ, NY, NX = 16, 4, 4
CHUNK = TOK // (2 * NX)

HIGHEST = lax.Precision.HIGHEST
EXP2_SCALE = QSCALE**-0.5 * 1.4426950408889634
BIG = 1e30
F32, BF16 = jnp.float32, jnp.bfloat16

PLAN = (1, 1, 2, 2, 2)


def nt(a, b, precision=None):
    return lax.dot_general(a, b, (((1,), (1,)), ((), ())), precision=precision, preferred_element_type=F32)


def nn(a, b, precision=None):
    return lax.dot_general(a, b, (((1,), (0,)), ((), ())), precision=precision, preferred_element_type=F32)


def orthonormal_rows(rows_list):
    nb = 8
    groups = RANK // nb
    lane_shape = (nb, 2 * RANK)
    sub = lax.broadcasted_iota(jnp.int32, lane_shape, 0)
    eye = (
        lax.broadcasted_iota(jnp.int32, (RANK, RANK), 0)
        == lax.broadcasted_iota(jnp.int32, (RANK, RANK), 1)
    ).astype(F32)
    tables = []
    for z in rows_list:
        both = jnp.concatenate([nt(z, z, HIGHEST), eye], axis=1)
        tables.append([both[nb * g : nb * g + nb] for g in range(groups)])
    for g0 in range(groups):
        k0 = nb * g0
        for table in tables:
            rows = [jnp.broadcast_to(table[g0][j : j + 1, :], lane_shape) for j in range(nb)]
            cols = [
                [jnp.broadcast_to(table[g][:, k0 + j : k0 + j + 1], lane_shape) for g in range(g0, groups)]
                for j in range(nb)
            ]
            inner = [
                [jnp.broadcast_to(cols[j][0][i : i + 1, :], lane_shape) if j >= i else None for j in range(nb)]
                for i in range(nb)
            ]
            pivots = []
            for j in range(nb):
                inv = lax.rsqrt(inner[j][j])
                row = rows[j] * inv
                col = [c * inv for c in cols[j]]
                pivots.append((row, col))
                factors = [inner[j][k] * inv if k >= j else None for k in range(nb)]
                for k in range(j + 1, nb):
                    rows[k] = rows[k] - factors[k] * row
                    cols[k] = [a - b * factors[k] for a, b in zip(cols[k], col)]
                    for m in range(k, nb):
                        inner[k][m] = inner[k][m] - factors[k] * factors[m]
            for at, g in enumerate(range(g0, groups)):
                x = table[g]
                for j, (row, col) in enumerate(pivots):
                    less = x - col[at] * row
                    x = jnp.where(sub > j, less, jnp.where(sub == j, row, x)) if g == g0 else less
                table[g] = x
    return [
        nn(jnp.concatenate(table, axis=0)[:, RANK:], z, HIGHEST) for table, z in zip(tables, rows_list)
    ]


def prepare_kernel(k_ref, v_ref, gram_ref, paired_ref):
    paired_ref[0] = k_ref[...]
    paired_ref[1] = v_ref[...]
    for h in range(gram_ref.shape[0]):
        k = k_ref[:, h * HD : (h + 1) * HD]
        gram_ref[h] = lax.dot_general(k, k, (((0,), (0,)), ((), ())), preferred_element_type=F32)


def prepare(keys, values):
    heads = keys.shape[1] // HD
    return pl.pallas_call(
        prepare_kernel,
        name="prepare",
        out_shape=[
            jax.ShapeDtypeStruct((heads, HD, HD), F32),
            jax.ShapeDtypeStruct((2,) + keys.shape, BF16),
        ],
        compiler_params=pltpu.CompilerParams(vmem_limit_bytes=8 << 20),
        cost_estimate=pl.CostEstimate(
            flops=2 * heads * TOK * HD * HD, bytes_accessed=8 * keys.size, transcendentals=0
        ),
    )(keys, values)


def iterate(gram_ref, start_ref, rows_ref, powers_ref):
    heads = start_ref.shape[0]
    row = lax.broadcasted_iota(jnp.int32, (HD, HD), 0)
    col = lax.broadcasted_iota(jnp.int32, (HD, HD), 1)
    for h in range(heads):
        gram = gram_ref[h]
        trace = jnp.sum(jnp.where(row == col, gram, 0.0))
        powers_ref[0, h] = gram
        powers_ref[1, h] = nn(gram, gram / trace, HIGHEST)
        rows_ref[h] = start_ref[h]
    singles = sum(1 for p in PLAN if p == 1)

    def step(i, carry):
        power = (i >= singles).astype(jnp.int32)
        moved = [nn(rows_ref[h], powers_ref[power, h], HIGHEST) for h in range(heads)]
        for h, rows in enumerate(orthonormal_rows(moved)):
            rows_ref[h] = rows
        return carry

    lax.fori_loop(0, len(PLAN), step, 0)


def attend(q, keys, vals, bias):
    row = lax.broadcasted_iota(jnp.int32, (QB, QB), 0)
    col = lax.broadcasted_iota(jnp.int32, (QB, QB), 1)
    old = col > row
    scores = [jnp.where(old, nt(q, keys[0]) + bias[0], nt(q, keys[4]))]
    scores += [nt(q, keys[b]) for b in (1, 2, 3)]
    peak = jnp.maximum(scores[0][:, :128], scores[0][:, 128:])
    for b in (1, 2, 3):
        peak = jnp.maximum(peak, jnp.maximum(scores[b][:, :128], scores[b][:, 128:]) + bias[b])
    peak = jnp.max(peak, axis=1, keepdims=True)
    edge = jnp.exp2((scores[0] - peak) * EXP2_SCALE)
    total = nn(jnp.where(old, edge, 0.0).astype(BF16), vals[0])
    total += nn(jnp.where(old, 0.0, edge).astype(BF16), vals[4])
    for b in (1, 2, 3):
        total += nn(jnp.exp2((scores[b] - (peak - bias[b])) * EXP2_SCALE).astype(BF16), vals[b])
    return total[:, :HD] / total[:, HD:]


def window_blocks(at_ref, k_ref, v_ref, near_ref, far_ref, lanes=slice(None)):
    first_valid = 4 - 2 * at_ref[0]
    ones = jnp.ones((QB, HD), BF16)
    keys, vals, bias = [], [], []
    for w in range(6):
        at = slice(w % 2 * QB, w % 2 * QB + QB)
        if w < 4:
            source = (far_ref, near_ref)[w // 2]
            key, val = source[0, at, lanes], source[1, at, lanes]
        else:
            key, val = k_ref[at, lanes], v_ref[at, lanes]
        keys.append(key)
        vals.append(jnp.concatenate([val, ones], axis=1))
        bias.append(jnp.where(w < first_valid, -BIG, 0.0).astype(F32))
    return keys, vals, bias


def tiles():
    for qb in range(TOK // QB):
        for j in range(2):
            yield qb, slice(qb * QB, (qb + 1) * QB), slice(j * HD, (j + 1) * HD)


def exact_kernel(at_ref, q_ref, k_ref, v_ref, near_ref, far_ref, out_ref):
    keys, vals, bias = window_blocks(at_ref, k_ref, v_ref, near_ref, far_ref)
    for qb, rows, cols in tiles():
        out_ref[rows, cols] = attend(q_ref[rows, cols], keys[qb : qb + 5], vals[qb : qb + 5], bias[qb:])


def approx_kernel(at_ref, gram_ref, start_ref, *refs):
    sources, outs, (rows_ref, powers_ref), held, sem = refs[:6], refs[6:9], refs[9:11], refs[11:17], refs[17]
    copies = [pltpu.make_async_copy(src, dst, sem.at[i]) for i, (src, dst) in enumerate(zip(sources, held))]
    for copy in copies:
        copy.start()
    iterate(gram_ref, start_ref, rows_ref, powers_ref)
    for copy in copies:
        copy.wait()
    q_ref, k_ref, v_ref, near_ref, far_ref, exact_ref = held
    low_ref, mine_ref, theirs_ref = outs
    for h in range(start_ref.shape[0]):
        lanes = slice(h * HD, (h + 1) * HD)
        keys, vals, bias = window_blocks(at_ref, k_ref, v_ref, near_ref, far_ref, lanes)
        basis = rows_ref[h].astype(BF16)
        keys = [nt(key, basis).astype(BF16) for key in keys]
        for qb, rows, cols in tiles():
            cols = slice(2 * h * HD + cols.start, 2 * h * HD + cols.stop)
            q = nt(q_ref[rows, cols], basis).astype(BF16)
            approx = attend(q, keys[qb : qb + 5], vals[qb : qb + 5], bias[qb:])
            low_ref[rows, cols] = approx.astype(BF16)
            gap = (exact_ref[rows, cols] - approx).astype(BF16)
            for i in range(QB // (2 * CHUNK)):
                first = gap[2 * i * CHUNK : (2 * i + 1) * CHUNK]
                second = gap[(2 * i + 1) * CHUNK : (2 * i + 2) * CHUNK]
                to = slice(qb * QB // 2 + i * CHUNK, qb * QB // 2 + (i + 1) * CHUNK)
                mine_ref[to, cols] = jnp.where(at_ref[1] == 0, first, second)
                theirs_ref[to, cols] = jnp.where(at_ref[1] == 0, second, first)


def approximate(at, gram, start, queries, keys, values, near, far, exact):
    heads = start.shape[0]
    whole = pl.BlockSpec(memory_space=pltpu.VMEM)
    left = pl.BlockSpec(memory_space=pl.ANY)
    sources = (queries, keys, values, near, far, exact)
    low = jax.ShapeDtypeStruct(queries.shape, BF16)
    half = jax.ShapeDtypeStruct((TOK // 2, queries.shape[1]), BF16)
    return pl.pallas_call(
        approx_kernel,
        name="approx",
        out_shape=[low, half, half],
        in_specs=[pl.BlockSpec(memory_space=pltpu.SMEM), whole, whole] + [left] * len(sources),
        out_specs=[whole] * 3,
        scratch_shapes=[pltpu.VMEM((heads, RANK, HD), F32), pltpu.VMEM((2, heads, HD, HD), F32)]
        + [pltpu.VMEM(source.shape, source.dtype) for source in sources]
        + [pltpu.SemaphoreType.DMA((len(sources),))],
        compiler_params=pltpu.CompilerParams(vmem_limit_bytes=24 << 20),
        cost_estimate=pl.CostEstimate(
            flops=4 * TOK * 1280 * 512 + 40_000_000, bytes_accessed=4 << 20, transcendentals=4 * TOK * 1024
        ),
    )(at, gram, start, *sources)


PAIR = pl.BlockSpec((TOK, 2 * HD), lambda h, at: (0, h))
ONE = pl.BlockSpec((TOK, HD), lambda h, at: (0, h))
BOTH = pl.BlockSpec((2, TOK, HD), lambda h, at: (0, 0, h))
WINDOW = [PAIR, ONE, ONE, BOTH, BOTH]


def attention(kernel, name, in_specs, out_specs, out_shape, operands):
    return pl.pallas_call(
        kernel,
        name=name,
        out_shape=out_shape,
        grid_spec=pltpu.PrefetchScalarGridSpec(
            num_scalar_prefetch=1,
            grid=(operands[2].shape[1] // HD,),
            in_specs=in_specs,
            out_specs=out_specs,
        ),
        compiler_params=pltpu.CompilerParams(vmem_limit_bytes=20 << 20),
        cost_estimate=pl.CostEstimate(
            flops=4 * TOK * 1280 * 512, bytes_accessed=4 << 20, transcendentals=4 * TOK * 1024
        ),
    )(*operands)


def project_kernel(mine_ref, theirs_ref, own_ref, other_ref, out_ref):
    total = nn(mine_ref[...], own_ref[...]) + nn(theirs_ref[...], other_ref[...])
    out_ref[...] = total.astype(BF16)


def project(mine, theirs, own, other):
    rows, feats = mine.shape
    width = own.shape[1]
    step = width // 3
    left = pl.BlockSpec((rows, feats), lambda n: (0, 0))
    right = pl.BlockSpec((feats, step), lambda n: (0, n))
    return pl.pallas_call(
        project_kernel,
        name="project",
        out_shape=jax.ShapeDtypeStruct((rows, width), BF16),
        grid=(width // step,),
        in_specs=[left, left, right, right],
        out_specs=pl.BlockSpec((rows, step), lambda n: (0, n)),
        compiler_params=pltpu.CompilerParams(vmem_limit_bytes=16 << 20),
        cost_estimate=pl.CostEstimate(
            flops=4 * rows * feats * width, bytes_accessed=4 * feats * width, transcendentals=0
        ),
    )(mine, theirs, own, other)


def shards(queries, keys, values, start_basis, out_weight):
    z, y, core = (lax.axis_index(name).astype(jnp.int32) for name in ("z", "y", "core"))
    seq = NZ * NY
    swap = [(0, 1), (1, 0)]
    in_place = lambda array: pltpu.with_memory_space_constraint(array, pltpu.HBM)
    held = (jnp.stack([z * NY + y, core]), *map(in_place, (queries, keys, values)))

    gram, paired = prepare(in_place(keys), in_place(values))
    shape = gram.shape
    gram = lax.all_to_all(gram.reshape(seq, -1, HD), ("z", "y"), 0, 0, tiled=True).sum(0)
    near = lax.ppermute(paired, ("z", "y"), [(i, i + 1) for i in range(seq - 1)])
    passed = lax.ppermute(paired, "y", [(i, (i - 1) % NY) for i in range(NY)])
    holder = lambda i: i - 1 if i % NY else i + NY - 1
    far = lax.ppermute(passed, ("z", "y"), [(holder(i), i + 2) for i in range(seq - 2)])
    other_weight = lax.ppermute(out_weight, "core", swap)
    gram = jnp.broadcast_to(gram[None], (seq,) + gram.shape)
    gram = lax.all_to_all(gram, ("z", "y"), 0, 0, tiled=True).reshape(shape)
    exact = attention(
        exact_kernel,
        "exact",
        WINDOW,
        PAIR,
        jax.ShapeDtypeStruct(queries.shape, F32),
        held + (near, far),
    )
    gram, exact = lax.optimization_barrier((gram, exact))
    lowrank_attn, mine, theirs = approximate(
        held[0], gram, start_basis.swapaxes(1, 2), *held[1:], *map(in_place, (near, far, exact))
    )

    theirs = lax.ppermute(theirs, "core", swap)
    partial = project(mine, theirs, out_weight, other_weight).reshape(NX, CHUNK, -1)
    partial = lax.all_to_all(partial, "x", 0, 0, tiled=True)
    return lowrank_attn, partial.astype(F32).sum(0).astype(BF16)


def solution(mesh):
    fine = Mesh(mesh.devices.reshape(NZ, NY, NX, 2), ("z", "y", "x", "core"))
    seq, head = ("z", "y"), ("x", "core")
    placed = (P(seq, head), P(seq, head), P(seq, head), P(head, None, None), P(head, None))
    return jax.shard_map(
        shards,
        mesh=fine,
        in_specs=placed,
        out_specs=(P(seq, head), P(seq + head, None)),
        check_vma=False,
    )
```

```python
import jax
import jax.numpy as jnp
from jax import lax
from jax.experimental import pallas as pl
from jax.experimental.pallas import tpu as pltpu
from jax.sharding import Mesh
from jax.sharding import PartitionSpec as P

HD = 128
QSCALE = 168
RANK = 64
TOK = 512
QB = 256
NZ, NY, NX = 16, 4, 4
CHUNK = TOK // (2 * NX)

HIGHEST = lax.Precision.HIGHEST
EXP2_SCALE = QSCALE**-0.5 * 1.4426950408889634
BIG = 1e30
F32, BF16 = jnp.float32, jnp.bfloat16

PLAN = (1, 1, 2, 2, 2)


def nt(a, b, precision=None):
    return lax.dot_general(a, b, (((1,), (1,)), ((), ())), precision=precision, preferred_element_type=F32)


def nn(a, b, precision=None):
    return lax.dot_general(a, b, (((1,), (0,)), ((), ())), precision=precision, preferred_element_type=F32)


def orthonormal_rows(rows_list):
    nb = 8
    groups = RANK // nb
    lane_shape = (nb, 2 * RANK)
    sub = lax.broadcasted_iota(jnp.int32, lane_shape, 0)
    eye = (
        lax.broadcasted_iota(jnp.int32, (RANK, RANK), 0)
        == lax.broadcasted_iota(jnp.int32, (RANK, RANK), 1)
    ).astype(F32)
    tables = []
    for z in rows_list:
        both = jnp.concatenate([nt(z, z, HIGHEST), eye], axis=1)
        tables.append([both[nb * g : nb * g + nb] for g in range(groups)])
    for g0 in range(groups):
        k0 = nb * g0
        for table in tables:
            rows = [jnp.broadcast_to(table[g0][j : j + 1, :], lane_shape) for j in range(nb)]
            cols = [
                [jnp.broadcast_to(table[g][:, k0 + j : k0 + j + 1], lane_shape) for g in range(g0, groups)]
                for j in range(nb)
            ]
            inner = [
                [jnp.broadcast_to(cols[j][0][i : i + 1, :], lane_shape) if j >= i else None for j in range(nb)]
                for i in range(nb)
            ]
            pivots = []
            for j in range(nb):
                inv = lax.rsqrt(inner[j][j])
                row = rows[j] * inv
                col = [c * inv for c in cols[j]]
                pivots.append((row, col))
                factors = [inner[j][k] * inv if k >= j else None for k in range(nb)]
                for k in range(j + 1, nb):
                    rows[k] = rows[k] - factors[k] * row
                    cols[k] = [a - b * factors[k] for a, b in zip(cols[k], col)]
                    for m in range(k, nb):
                        inner[k][m] = inner[k][m] - factors[k] * factors[m]
            for at, g in enumerate(range(g0, groups)):
                x = table[g]
                for j, (row, col) in enumerate(pivots):
                    less = x - col[at] * row
                    x = jnp.where(sub > j, less, jnp.where(sub == j, row, x)) if g == g0 else less
                table[g] = x
    return [
        nn(jnp.concatenate(table, axis=0)[:, RANK:], z, HIGHEST) for table, z in zip(tables, rows_list)
    ]


def prepare_kernel(k_ref, v_ref, gram_ref, paired_ref):
    paired_ref[0] = k_ref[...]
    paired_ref[1] = v_ref[...]
    for h in range(gram_ref.shape[0]):
        k = k_ref[:, h * HD : (h + 1) * HD]
        gram_ref[h] = lax.dot_general(k, k, (((0,), (0,)), ((), ())), preferred_element_type=F32)


def prepare(keys, values):
    heads = keys.shape[1] // HD
    return pl.pallas_call(
        prepare_kernel,
        name="prepare",
        out_shape=[
            jax.ShapeDtypeStruct((heads, HD, HD), F32),
            jax.ShapeDtypeStruct((2,) + keys.shape, BF16),
        ],
        compiler_params=pltpu.CompilerParams(vmem_limit_bytes=8 << 20),
        cost_estimate=pl.CostEstimate(
            flops=2 * heads * TOK * HD * HD, bytes_accessed=8 * keys.size, transcendentals=0
        ),
    )(keys, values)


def iterate(gram_ref, start_ref, rows_ref, powers_ref):
    heads = start_ref.shape[0]
    row = lax.broadcasted_iota(jnp.int32, (HD, HD), 0)
    col = lax.broadcasted_iota(jnp.int32, (HD, HD), 1)
    for h in range(heads):
        gram = gram_ref[h]
        trace = jnp.sum(jnp.where(row == col, gram, 0.0))
        powers_ref[0, h] = gram
        powers_ref[1, h] = nn(gram, gram / trace, HIGHEST)
        rows_ref[h] = start_ref[h]
    singles = sum(1 for p in PLAN if p == 1)

    def step(i, carry):
        power = (i >= singles).astype(jnp.int32)
        moved = [nn(rows_ref[h], powers_ref[power, h], HIGHEST) for h in range(heads)]
        for h, rows in enumerate(orthonormal_rows(moved)):
            rows_ref[h] = rows
        return carry

    lax.fori_loop(0, len(PLAN), step, 0)


def attend(q, keys, vals, bias):
    row = lax.broadcasted_iota(jnp.int32, (QB, QB), 0)
    col = lax.broadcasted_iota(jnp.int32, (QB, QB), 1)
    old = col > row
    scores = [jnp.where(old, nt(q, keys[0]) + bias[0], nt(q, keys[4]))]
    scores += [nt(q, keys[b]) for b in (1, 2, 3)]
    peak = jnp.maximum(scores[0][:, :128], scores[0][:, 128:])
    for b in (1, 2, 3):
        peak = jnp.maximum(peak, jnp.maximum(scores[b][:, :128], scores[b][:, 128:]) + bias[b])
    peak = jnp.max(peak, axis=1, keepdims=True)
    edge = jnp.exp2((scores[0] - peak) * EXP2_SCALE)
    total = nn(jnp.where(old, edge, 0.0).astype(BF16), vals[0])
    total += nn(jnp.where(old, 0.0, edge).astype(BF16), vals[4])
    for b in (1, 2, 3):
        total += nn(jnp.exp2((scores[b] - (peak - bias[b])) * EXP2_SCALE).astype(BF16), vals[b])
    return total[:, :HD] / total[:, HD:]


def window_blocks(at_ref, k_ref, v_ref, near_ref, far_ref, lanes=slice(None)):
    first_valid = 4 - 2 * at_ref[0]
    ones = jnp.ones((QB, HD), BF16)
    keys, vals, bias = [], [], []
    for w in range(6):
        at = slice(w % 2 * QB, w % 2 * QB + QB)
        if w < 4:
            source = (far_ref, near_ref)[w // 2]
            key, val = source[0, at, lanes], source[1, at, lanes]
        else:
            key, val = k_ref[at, lanes], v_ref[at, lanes]
        keys.append(key)
        vals.append(jnp.concatenate([val, ones], axis=1))
        bias.append(jnp.where(w < first_valid, -BIG, 0.0).astype(F32))
    return keys, vals, bias


def tiles():
    for qb in range(TOK // QB):
        for j in range(2):
            yield qb, slice(qb * QB, (qb + 1) * QB), slice(j * HD, (j + 1) * HD)


def exact_kernel(at_ref, q_ref, k_ref, v_ref, near_ref, far_ref, out_ref):
    keys, vals, bias = window_blocks(at_ref, k_ref, v_ref, near_ref, far_ref)
    for qb, rows, cols in tiles():
        out_ref[rows, cols] = attend(q_ref[rows, cols], keys[qb : qb + 5], vals[qb : qb + 5], bias[qb:])


def approx_kernel(at_ref, gram_ref, start_ref, *refs):
    sources, outs, (rows_ref, powers_ref), held, sem = refs[:6], refs[6:9], refs[9:11], refs[11:17], refs[17]
    copies = [pltpu.make_async_copy(src, dst, sem.at[i]) for i, (src, dst) in enumerate(zip(sources, held))]
    for copy in copies:
        copy.start()
    iterate(gram_ref, start_ref, rows_ref, powers_ref)
    for copy in copies:
        copy.wait()
    q_ref, k_ref, v_ref, near_ref, far_ref, exact_ref = held
    low_ref, mine_ref, theirs_ref = outs
    for h in range(start_ref.shape[0]):
        lanes = slice(h * HD, (h + 1) * HD)
        keys, vals, bias = window_blocks(at_ref, k_ref, v_ref, near_ref, far_ref, lanes)
        basis = rows_ref[h].astype(BF16)
        keys = [nt(key, basis).astype(BF16) for key in keys]
        for qb, rows, cols in tiles():
            cols = slice(2 * h * HD + cols.start, 2 * h * HD + cols.stop)
            q = nt(q_ref[rows, cols], basis).astype(BF16)
            approx = attend(q, keys[qb : qb + 5], vals[qb : qb + 5], bias[qb:])
            low_ref[rows, cols] = approx.astype(BF16)
            gap = (exact_ref[rows, cols] - approx).astype(BF16)
            for i in range(QB // (2 * CHUNK)):
                first = gap[2 * i * CHUNK : (2 * i + 1) * CHUNK]
                second = gap[(2 * i + 1) * CHUNK : (2 * i + 2) * CHUNK]
                to = slice(qb * QB // 2 + i * CHUNK, qb * QB // 2 + (i + 1) * CHUNK)
                mine_ref[to, cols] = jnp.where(at_ref[1] == 0, first, second)
                theirs_ref[to, cols] = jnp.where(at_ref[1] == 0, second, first)


def approximate(at, gram, start, queries, keys, values, near, far, exact):
    heads = start.shape[0]
    whole = pl.BlockSpec(memory_space=pltpu.VMEM)
    left = pl.BlockSpec(memory_space=pl.ANY)
    sources = (queries, keys, values, near, far, exact)
    low = jax.ShapeDtypeStruct(queries.shape, BF16)
    half = jax.ShapeDtypeStruct((TOK // 2, queries.shape[1]), BF16)
    return pl.pallas_call(
        approx_kernel,
        name="approx",
        out_shape=[low, half, half],
        in_specs=[pl.BlockSpec(memory_space=pltpu.SMEM), whole, whole] + [left] * len(sources),
        out_specs=[whole] * 3,
        scratch_shapes=[pltpu.VMEM((heads, RANK, HD), F32), pltpu.VMEM((2, heads, HD, HD), F32)]
        + [pltpu.VMEM(source.shape, source.dtype) for source in sources]
        + [pltpu.SemaphoreType.DMA((len(sources),))],
        compiler_params=pltpu.CompilerParams(vmem_limit_bytes=24 << 20),
        cost_estimate=pl.CostEstimate(
            flops=4 * TOK * 1280 * 512 + 40_000_000, bytes_accessed=4 << 20, transcendentals=4 * TOK * 1024
        ),
    )(at, gram, start, *sources)


PAIR = pl.BlockSpec((TOK, 2 * HD), lambda h, at: (0, h))
ONE = pl.BlockSpec((TOK, HD), lambda h, at: (0, h))
BOTH = pl.BlockSpec((2, TOK, HD), lambda h, at: (0, 0, h))
WINDOW = [PAIR, ONE, ONE, BOTH, BOTH]


def attention(kernel, name, in_specs, out_specs, out_shape, operands):
    return pl.pallas_call(
        kernel,
        name=name,
        out_shape=out_shape,
        grid_spec=pltpu.PrefetchScalarGridSpec(
            num_scalar_prefetch=1,
            grid=(operands[2].shape[1] // HD,),
            in_specs=in_specs,
            out_specs=out_specs,
        ),
        compiler_params=pltpu.CompilerParams(vmem_limit_bytes=20 << 20),
        cost_estimate=pl.CostEstimate(
            flops=4 * TOK * 1280 * 512, bytes_accessed=4 << 20, transcendentals=4 * TOK * 1024
        ),
    )(*operands)


def project_kernel(rows_ref, weight_ref, *refs):
    total = nn(rows_ref[...], weight_ref[...])
    if len(refs) == 2:
        total += refs[0][...]
    refs[-1][...] = total.astype(refs[-1].dtype)


def project(rows, weight, name, dtype, *added):
    count, feats = rows.shape
    width = weight.shape[1]
    step = width // 3
    part = pl.BlockSpec((count, step), lambda n: (0, n))
    return pl.pallas_call(
        project_kernel,
        name=name,
        out_shape=jax.ShapeDtypeStruct((count, width), dtype),
        grid=(width // step,),
        in_specs=[
            pl.BlockSpec((count, feats), lambda n: (0, 0)),
            pl.BlockSpec((feats, step), lambda n: (0, n)),
        ]
        + [part] * len(added),
        out_specs=part,
        compiler_params=pltpu.CompilerParams(vmem_limit_bytes=12 << 20),
        cost_estimate=pl.CostEstimate(
            flops=2 * count * feats * width, bytes_accessed=4 * feats * width, transcendentals=0
        ),
    )(rows, weight, *added)


def shards(queries, keys, values, start_basis, out_weight):
    z, y, core = (lax.axis_index(name).astype(jnp.int32) for name in ("z", "y", "core"))
    seq = NZ * NY
    swap = [(0, 1), (1, 0)]
    in_place = lambda array: pltpu.with_memory_space_constraint(array, pltpu.HBM)
    held = (jnp.stack([z * NY + y, core]), *map(in_place, (queries, keys, values)))

    gram, paired = prepare(in_place(keys), in_place(values))
    shape = gram.shape
    gram = lax.all_to_all(gram.reshape(seq, -1, HD), ("z", "y"), 0, 0, tiled=True).sum(0)
    near = lax.ppermute(paired, ("z", "y"), [(i, i + 1) for i in range(seq - 1)])
    passed = lax.ppermute(paired, "y", [(i, (i - 1) % NY) for i in range(NY)])
    holder = lambda i: i - 1 if i % NY else i + NY - 1
    far = lax.ppermute(passed, ("z", "y"), [(holder(i), i + 2) for i in range(seq - 2)])
    other_weight = lax.ppermute(out_weight, "core", swap)
    gram = jnp.broadcast_to(gram[None], (seq,) + gram.shape)
    gram = lax.all_to_all(gram, ("z", "y"), 0, 0, tiled=True).reshape(shape)
    exact = attention(
        exact_kernel,
        "exact",
        WINDOW,
        PAIR,
        jax.ShapeDtypeStruct(queries.shape, F32),
        held + (near, far),
    )
    gram, exact = lax.optimization_barrier((gram, exact))
    lowrank_attn, mine, theirs = approximate(
        held[0], gram, start_basis.swapaxes(1, 2), *held[1:], *map(in_place, (near, far, exact))
    )

    theirs = lax.ppermute(theirs, "core", swap)
    partial = project(mine, out_weight, "project_mine", F32)
    partial = project(theirs, other_weight, "project_theirs", BF16, partial).reshape(NX, CHUNK, -1)
    partial = lax.all_to_all(partial, "x", 0, 0, tiled=True)
    return lowrank_attn, partial.astype(F32).sum(0).astype(BF16)


def solution(mesh):
    fine = Mesh(mesh.devices.reshape(NZ, NY, NX, 2), ("z", "y", "x", "core"))
    seq, head = ("z", "y"), ("x", "core")
    placed = (P(seq, head), P(seq, head), P(seq, head), P(head, None, None), P(head, None))
    return jax.shard_map(
        shards,
        mesh=fine,
        in_specs=placed,
        out_specs=(P(seq, head), P(seq + head, None)),
        check_vma=False,
    )
```

```python
import jax
import jax.numpy as jnp
from jax import lax
from jax.experimental import pallas as pl
from jax.experimental.pallas import tpu as pltpu
from jax.sharding import Mesh
from jax.sharding import PartitionSpec as P

HD = 128
QSCALE = 168
RANK = 64
TOK = 512
QB = 256
NZ, NY, NX = 16, 4, 4
CHUNK = TOK // (2 * NX)

HIGHEST = lax.Precision.HIGHEST
EXP2_SCALE = QSCALE**-0.5 * 1.4426950408889634
BIG = 1e30
F32, BF16 = jnp.float32, jnp.bfloat16

PLAN = (1, 1, 2, 2, 2)


def nt(a, b, precision=None):
    return lax.dot_general(a, b, (((1,), (1,)), ((), ())), precision=precision, preferred_element_type=F32)


def nn(a, b, precision=None):
    return lax.dot_general(a, b, (((1,), (0,)), ((), ())), precision=precision, preferred_element_type=F32)


def orthonormal_rows(rows_list):
    nb = 8
    groups = RANK // nb
    lane_shape = (nb, 2 * RANK)
    sub = lax.broadcasted_iota(jnp.int32, lane_shape, 0)
    eye = (
        lax.broadcasted_iota(jnp.int32, (RANK, RANK), 0)
        == lax.broadcasted_iota(jnp.int32, (RANK, RANK), 1)
    ).astype(F32)
    tables = []
    for z in rows_list:
        both = jnp.concatenate([nt(z, z, HIGHEST), eye], axis=1)
        tables.append([both[nb * g : nb * g + nb] for g in range(groups)])
    for g0 in range(groups):
        k0 = nb * g0
        for table in tables:
            rows = [jnp.broadcast_to(table[g0][j : j + 1, :], lane_shape) for j in range(nb)]
            cols = [
                [jnp.broadcast_to(table[g][:, k0 + j : k0 + j + 1], lane_shape) for g in range(g0, groups)]
                for j in range(nb)
            ]
            inner = [
                [jnp.broadcast_to(cols[j][0][i : i + 1, :], lane_shape) if j >= i else None for j in range(nb)]
                for i in range(nb)
            ]
            pivots = []
            for j in range(nb):
                inv = lax.rsqrt(inner[j][j])
                row = rows[j] * inv
                col = [c * inv for c in cols[j]]
                pivots.append((row, col))
                factors = [inner[j][k] * inv if k >= j else None for k in range(nb)]
                for k in range(j + 1, nb):
                    rows[k] = rows[k] - factors[k] * row
                    cols[k] = [a - b * factors[k] for a, b in zip(cols[k], col)]
                    for m in range(k, nb):
                        inner[k][m] = inner[k][m] - factors[k] * factors[m]
            for at, g in enumerate(range(g0, groups)):
                x = table[g]
                for j, (row, col) in enumerate(pivots):
                    less = x - col[at] * row
                    x = jnp.where(sub > j, less, jnp.where(sub == j, row, x)) if g == g0 else less
                table[g] = x
    return [
        nn(jnp.concatenate(table, axis=0)[:, RANK:], z, HIGHEST) for table, z in zip(tables, rows_list)
    ]


def prepare_kernel(k_ref, v_ref, gram_ref, paired_ref):
    paired_ref[0] = k_ref[...]
    paired_ref[1] = v_ref[...]
    for h in range(gram_ref.shape[0]):
        k = k_ref[:, h * HD : (h + 1) * HD]
        gram_ref[h] = lax.dot_general(k, k, (((0,), (0,)), ((), ())), preferred_element_type=F32)


def prepare(keys, values):
    heads = keys.shape[1] // HD
    return pl.pallas_call(
        prepare_kernel,
        name="prepare",
        out_shape=[
            jax.ShapeDtypeStruct((heads, HD, HD), F32),
            jax.ShapeDtypeStruct((2,) + keys.shape, BF16),
        ],
        compiler_params=pltpu.CompilerParams(vmem_limit_bytes=8 << 20),
        cost_estimate=pl.CostEstimate(
            flops=2 * heads * TOK * HD * HD, bytes_accessed=8 * keys.size, transcendentals=0
        ),
    )(keys, values)


def add_up_kernel(parts_ref, out_ref):
    out_ref[...] = jnp.broadcast_to(jnp.sum(parts_ref[...], axis=0, keepdims=True), out_ref.shape)


def add_up(parts):
    return pl.pallas_call(
        add_up_kernel,
        name="add_up",
        out_shape=jax.ShapeDtypeStruct(parts.shape, F32),
        compiler_params=pltpu.CompilerParams(vmem_limit_bytes=4 << 20),
    )(parts)


def iterate(gram_ref, start_ref, rows_ref, powers_ref):
    heads = start_ref.shape[0]
    row = lax.broadcasted_iota(jnp.int32, (HD, HD), 0)
    col = lax.broadcasted_iota(jnp.int32, (HD, HD), 1)
    for h in range(heads):
        gram = gram_ref[h]
        trace = jnp.sum(jnp.where(row == col, gram, 0.0))
        powers_ref[0, h] = gram
        powers_ref[1, h] = nn(gram, gram / trace, HIGHEST)
        rows_ref[h] = start_ref[h]
    singles = sum(1 for p in PLAN if p == 1)

    def step(i, carry):
        power = (i >= singles).astype(jnp.int32)
        moved = [nn(rows_ref[h], powers_ref[power, h], HIGHEST) for h in range(heads)]
        for h, rows in enumerate(orthonormal_rows(moved)):
            rows_ref[h] = rows
        return carry

    lax.fori_loop(0, len(PLAN), step, 0)


def attend(q, keys, vals, bias):
    row = lax.broadcasted_iota(jnp.int32, (QB, QB), 0)
    col = lax.broadcasted_iota(jnp.int32, (QB, QB), 1)
    old = col > row
    scores = [jnp.where(old, nt(q, keys[0]) + bias[0], nt(q, keys[4]))]
    scores += [nt(q, keys[b]) for b in (1, 2, 3)]
    peak = jnp.maximum(scores[0][:, :128], scores[0][:, 128:])
    for b in (1, 2, 3):
        peak = jnp.maximum(peak, jnp.maximum(scores[b][:, :128], scores[b][:, 128:]) + bias[b])
    peak = jnp.max(peak, axis=1, keepdims=True)
    edge = jnp.exp2((scores[0] - peak) * EXP2_SCALE)
    total = nn(jnp.where(old, edge, 0.0).astype(BF16), vals[0])
    total += nn(jnp.where(old, 0.0, edge).astype(BF16), vals[4])
    for b in (1, 2, 3):
        total += nn(jnp.exp2((scores[b] - (peak - bias[b])) * EXP2_SCALE).astype(BF16), vals[b])
    return total[:, :HD] / total[:, HD:]


def window_blocks(at_ref, k_ref, v_ref, near_ref, far_ref, lanes=slice(None)):
    first_valid = 4 - 2 * at_ref[0]
    ones = jnp.ones((QB, HD), BF16)
    keys, vals, bias = [], [], []
    for w in range(6):
        at = slice(w % 2 * QB, w % 2 * QB + QB)
        if w < 4:
            source = (far_ref, near_ref)[w // 2]
            key, val = source[0, at, lanes], source[1, at, lanes]
        else:
            key, val = k_ref[at, lanes], v_ref[at, lanes]
        keys.append(key)
        vals.append(jnp.concatenate([val, ones], axis=1))
        bias.append(jnp.where(w < first_valid, -BIG, 0.0).astype(F32))
    return keys, vals, bias


def tiles():
    for qb in range(TOK // QB):
        for j in range(2):
            yield qb, slice(qb * QB, (qb + 1) * QB), slice(j * HD, (j + 1) * HD)


def exact_kernel(at_ref, q_ref, k_ref, v_ref, near_ref, far_ref, out_ref):
    keys, vals, bias = window_blocks(at_ref, k_ref, v_ref, near_ref, far_ref)
    for qb, rows, cols in tiles():
        out_ref[rows, cols] = attend(q_ref[rows, cols], keys[qb : qb + 5], vals[qb : qb + 5], bias[qb:])


def approx_kernel(at_ref, gram_ref, start_ref, *refs):
    sources, outs, (rows_ref, powers_ref), held, sem = refs[:6], refs[6:9], refs[9:11], refs[11:17], refs[17]
    copies = [pltpu.make_async_copy(src, dst, sem.at[i]) for i, (src, dst) in enumerate(zip(sources, held))]
    for copy in copies:
        copy.start()
    iterate(gram_ref, start_ref, rows_ref, powers_ref)
    for copy in copies:
        copy.wait()
    q_ref, k_ref, v_ref, near_ref, far_ref, exact_ref = held
    low_ref, mine_ref, theirs_ref = outs
    for h in range(start_ref.shape[0]):
        lanes = slice(h * HD, (h + 1) * HD)
        keys, vals, bias = window_blocks(at_ref, k_ref, v_ref, near_ref, far_ref, lanes)
        basis = rows_ref[h].astype(BF16)
        keys = [nt(key, basis).astype(BF16) for key in keys]
        for qb, rows, cols in tiles():
            cols = slice(2 * h * HD + cols.start, 2 * h * HD + cols.stop)
            q = nt(q_ref[rows, cols], basis).astype(BF16)
            approx = attend(q, keys[qb : qb + 5], vals[qb : qb + 5], bias[qb:])
            low_ref[rows, cols] = approx.astype(BF16)
            gap = (exact_ref[rows, cols] - approx).astype(BF16)
            for i in range(QB // (2 * CHUNK)):
                first = gap[2 * i * CHUNK : (2 * i + 1) * CHUNK]
                second = gap[(2 * i + 1) * CHUNK : (2 * i + 2) * CHUNK]
                to = slice(qb * QB // 2 + i * CHUNK, qb * QB // 2 + (i + 1) * CHUNK)
                mine_ref[to, cols] = jnp.where(at_ref[1] == 0, first, second)
                theirs_ref[to, cols] = jnp.where(at_ref[1] == 0, second, first)


def approximate(at, gram, start, queries, keys, values, near, far, exact):
    heads = start.shape[0]
    whole = pl.BlockSpec(memory_space=pltpu.VMEM)
    left = pl.BlockSpec(memory_space=pl.ANY)
    sources = (queries, keys, values, near, far, exact)
    low = jax.ShapeDtypeStruct(queries.shape, BF16)
    half = jax.ShapeDtypeStruct((TOK // 2, queries.shape[1]), BF16)
    return pl.pallas_call(
        approx_kernel,
        name="approx",
        out_shape=[low, half, half],
        in_specs=[pl.BlockSpec(memory_space=pltpu.SMEM), whole, whole] + [left] * len(sources),
        out_specs=[whole] * 3,
        scratch_shapes=[pltpu.VMEM((heads, RANK, HD), F32), pltpu.VMEM((2, heads, HD, HD), F32)]
        + [pltpu.VMEM(source.shape, source.dtype) for source in sources]
        + [pltpu.SemaphoreType.DMA((len(sources),))],
        compiler_params=pltpu.CompilerParams(vmem_limit_bytes=24 << 20),
        cost_estimate=pl.CostEstimate(
            flops=4 * TOK * 1280 * 512 + 40_000_000, bytes_accessed=4 << 20, transcendentals=4 * TOK * 1024
        ),
    )(at, gram, start, *sources)


PAIR = pl.BlockSpec((TOK, 2 * HD), lambda h, at: (0, h))
ONE = pl.BlockSpec((TOK, HD), lambda h, at: (0, h))
BOTH = pl.BlockSpec((2, TOK, HD), lambda h, at: (0, 0, h))
WINDOW = [PAIR, ONE, ONE, BOTH, BOTH]


def attention(kernel, name, in_specs, out_specs, out_shape, operands):
    return pl.pallas_call(
        kernel,
        name=name,
        out_shape=out_shape,
        grid_spec=pltpu.PrefetchScalarGridSpec(
            num_scalar_prefetch=1,
            grid=(operands[2].shape[1] // HD,),
            in_specs=in_specs,
            out_specs=out_specs,
        ),
        compiler_params=pltpu.CompilerParams(vmem_limit_bytes=20 << 20),
        cost_estimate=pl.CostEstimate(
            flops=4 * TOK * 1280 * 512, bytes_accessed=4 << 20, transcendentals=4 * TOK * 1024
        ),
    )(*operands)


def project_kernel(rows_ref, weight_ref, *refs):
    total = nn(rows_ref[...], weight_ref[...])
    if len(refs) == 2:
        total += refs[0][...]
    refs[-1][...] = total.astype(refs[-1].dtype)


def project(rows, weight, name, dtype, *added):
    count, feats = rows.shape
    width = weight.shape[1]
    step = width // 3
    part = pl.BlockSpec((count, step), lambda n: (0, n))
    return pl.pallas_call(
        project_kernel,
        name=name,
        out_shape=jax.ShapeDtypeStruct((count, width), dtype),
        grid=(width // step,),
        in_specs=[
            pl.BlockSpec((count, feats), lambda n: (0, 0)),
            pl.BlockSpec((feats, step), lambda n: (0, n)),
        ]
        + [part] * len(added),
        out_specs=part,
        compiler_params=pltpu.CompilerParams(vmem_limit_bytes=12 << 20),
        cost_estimate=pl.CostEstimate(
            flops=2 * count * feats * width, bytes_accessed=4 * feats * width, transcendentals=0
        ),
    )(rows, weight, *added)


def shards(queries, keys, values, start_basis, out_weight):
    z, y, core = (lax.axis_index(name).astype(jnp.int32) for name in ("z", "y", "core"))
    seq = NZ * NY
    swap = [(0, 1), (1, 0)]
    in_place = lambda array: pltpu.with_memory_space_constraint(array, pltpu.HBM)
    held = (jnp.stack([z * NY + y, core]), *map(in_place, (queries, keys, values)))

    gram, paired = prepare(in_place(keys), in_place(values))
    shape = gram.shape
    gram = lax.all_to_all(gram.reshape(seq, -1, HD), ("z", "y"), 0, 0, tiled=True)
    near = lax.ppermute(paired, ("z", "y"), [(i, i + 1) for i in range(seq - 1)])
    passed = lax.ppermute(paired, "y", [(i, (i - 1) % NY) for i in range(NY)])
    holder = lambda i: i - 1 if i % NY else i + NY - 1
    far = lax.ppermute(passed, ("z", "y"), [(holder(i), i + 2) for i in range(seq - 2)])
    other_weight = lax.ppermute(out_weight, "core", swap)
    gram = add_up(gram)
    gram = lax.all_to_all(gram, ("z", "y"), 0, 0, tiled=True).reshape(shape)
    exact = attention(
        exact_kernel,
        "exact",
        WINDOW,
        PAIR,
        jax.ShapeDtypeStruct(queries.shape, F32),
        held + (near, far),
    )
    gram, exact = lax.optimization_barrier((gram, exact))
    lowrank_attn, mine, theirs = approximate(
        held[0], gram, start_basis.swapaxes(1, 2), *held[1:], *map(in_place, (near, far, exact))
    )

    theirs = lax.ppermute(theirs, "core", swap)
    partial = project(mine, out_weight, "project_mine", F32)
    partial = project(theirs, other_weight, "project_theirs", BF16, partial).reshape(NX, CHUNK, -1)
    partial = lax.all_to_all(partial, "x", 0, 0, tiled=True)
    return lowrank_attn, partial.astype(F32).sum(0).astype(BF16)


def solution(mesh):
    fine = Mesh(mesh.devices.reshape(NZ, NY, NX, 2), ("z", "y", "x", "core"))
    seq, head = ("z", "y"), ("x", "core")
    placed = (P(seq, head), P(seq, head), P(seq, head), P(head, None, None), P(head, None))
    return jax.shard_map(
        shards,
        mesh=fine,
        in_specs=placed,
        out_specs=(P(seq, head), P(seq + head, None)),
        check_vma=False,
    )
```
